32 devices in a mesh: outer: 2 (over x), inner: 16 (over z, y, core).
Axes of the slice: x: 2, y: 2, z: 4, core: 2. Of those that a mesh axis runs over, the one named last changes fastest.
Arguments:
- points: bfloat16 [16, 131072], P(None, ('outer', 'inner')), may hold values from -3 to 3
- charges: bfloat16 [64, 131072], P(None, ('outer', 'inner')), may hold values from -6 to 6
- near_leaves: int32 [512, 16], P(('outer', 'inner')), may hold values from 0 to 511, as said below
- skel_device: int32 [32, 512], P(('outer', 'inner')), may hold values from 0 to 4095, as said below
- skel_tree: int32 [32, 4, 512], P(('outer', 'inner')), may hold values from 0 to 1023, as said below
Outputs:
- potential: float32 [64, 131072], P(None, ('outer', 'inner'))
The draws below stay inside these ranges and needn't reach their ends.
Inputs may be any that keep to these rules, and one draw needn't show every extreme that they name: `near_leaves`: row b holds 16 different leaf numbers, b among them, each a leaf of b's level-0 node or of the level-0 nodes just before and just after it. `skel_device`: row c holds 512 different offsets among the 4096 points of level-0 node c. skel_tree[c, k] holds 512 different positions among the 1024 skeleton points of the children of the level-(k+1) node that contains level-0 node c; all level-0 nodes inside one level-(k+1) node have equal rows k.
All inputs are finite; a program needn't handle non-finite values.
Results may differ from the reference program's by a relative error of at most 0.0035.
Values may be sent and summed in bfloat16 or wider, within the bound.
A program may use at most 64 MiB of HBM per device.

```python
import jax
import jax.numpy as jnp
from jax import lax

DIM = 16
NRHS = 64
LEAF = 256
R = 512
NNEAR = 16
LEAF_DEV = 16
NODES = 32
NDEV = 4096
NLEAVES = 512
NPTS = 131072
LEVELS = 5


def draw_points(key, part):

    def unit_terms(salt, count):
        sub_key = jax.random.fold_in(key, salt)
        return jnp.clip(jax.random.normal(sub_key, (DIM, count), jnp.float32), -4.0, 4.0)
    total = 0.53 * unit_terms(1, NPTS)
    total = total + 0.32 * jnp.repeat(unit_terms(2, NLEAVES), LEAF, axis=1)
    for height in range(LEVELS):
        groups = NODES >> height
        factor = 0.6 if height == 0 else 0.38
        total = total + factor * jnp.repeat(unit_terms(3 + height, groups), NPTS // groups, axis=1)
    return jnp.clip(total, -3.0, 3.0).astype(jnp.bfloat16)


def draw_near_leaves(key, part):
    window = 3 * LEAF_DEV
    leaf_ids = jnp.arange(NLEAVES, dtype=jnp.int32)
    offsets = jnp.arange(window, dtype=jnp.int32)
    first = (leaf_ids // LEAF_DEV - 1) * LEAF_DEV
    candidate = first[:, None] + offsets[None, :]
    inside = (candidate >= 0) & (candidate < NLEAVES)
    scores = jax.random.randint(key, (NLEAVES, window), 0, 2 ** 20, dtype=jnp.int32) * window + offsets[None, :]
    scores = jnp.where(candidate == leaf_ids[:, None], 2 ** 30, scores)
    scores = jnp.where(inside, scores, -1)
    ranked, picked = lax.top_k(scores, NNEAR)
    return jnp.take_along_axis(candidate, picked, axis=1).astype(jnp.int32)


def draw_skel_device(key, part):

    def one_node(node_id):
        return jax.random.permutation(jax.random.fold_in(key, node_id), NDEV)[:R]
    return jax.vmap(one_node)(jnp.arange(NODES, dtype=jnp.int32)).astype(jnp.int32)


def draw_skel_tree(key, part):
    base_key = jax.random.fold_in(key, 91)
    layers = []
    for height in range(LEVELS - 1):
        groups = NODES >> height + 1
        layer_key = jax.random.fold_in(base_key, height)

        def one_group(group_id):
            return jax.random.permutation(jax.random.fold_in(layer_key, group_id), 2 * R)[:R]
        chosen = jax.vmap(one_group)(jnp.arange(groups, dtype=jnp.int32))
        layers.append(jnp.repeat(chosen, 2 ** (height + 1), axis=0))
    return jnp.stack(layers, axis=1).astype(jnp.int32)


def block_levels(own_key, extent, split, low, largest):
    def one(position, blocks):
        draws = jax.random.uniform(jax.random.fold_in(jax.random.fold_in(own_key, 6), position), (blocks,), jnp.float32, low / len(split), largest / len(split))
        return jnp.repeat(jnp.exp(draws), extent[position] // blocks).reshape((-1,) + (1,) * (len(extent) - position - 1))

    loudness = one(*split[0])
    for cut in split[1:]:
        loudness = loudness * one(*cut)
    return loudness


def normal_values(own_key, dims, deviation, reach, cuts=(), held_as=jnp.bfloat16):
    drawn = jax.random.normal(own_key, dims, jnp.float32) * deviation
    if len(cuts) > 0:
        drawn = block_levels(own_key, dims, cuts, -0.22, 0.18) * drawn
    return jnp.clip(drawn, min=-reach, max=reach).astype(held_as)


def setup_inputs(seed: int = 0) -> dict:
    splits = jax.random.split(jax.random.key(seed), 6)
    return {
        "points": draw_points(jax.random.fold_in(splits[5], 71), 0),
        "charges": normal_values(splits[1], (NRHS, NPTS), 1.0, 6.0, ((1, 32),)),
        "near_leaves": draw_near_leaves(jax.random.fold_in(splits[5], 71), 0),
        "skel_device": draw_skel_device(jax.random.fold_in(splits[5], 71), 0),
        "skel_tree": draw_skel_tree(jax.random.fold_in(splits[5], 71), 0),
    }


GAMMA = 0.125


def kernel_block(left, right):
    left32 = left.astype(jnp.float32)
    right32 = right.astype(jnp.float32)
    products = jnp.einsum("dm,dn->mn", left32, right32, precision=lax.Precision.HIGHEST)
    distance = jnp.sum(left32 * left32, 0)[:, None] + jnp.sum(right32 * right32, 0)[None, :] - 2.0 * products
    return jnp.exp(-GAMMA * distance).astype(jnp.bfloat16)


def spread_weights(weights, block):
    totals = jnp.sum(block.astype(jnp.float32), 1)
    return (weights.astype(jnp.float32) / totals[None, :]).astype(jnp.bfloat16)


def carry_values(values, block):
    totals = jnp.sum(block.astype(jnp.float32), 0)
    return jnp.dot(values, block, preferred_element_type=jnp.float32) / totals[None, :]


def parent_node(joined, chosen):
    joined_x = joined[:DIM]
    parent_x = jnp.take(joined_x, chosen, axis=1)
    block = kernel_block(joined_x, parent_x)
    parent_up = jnp.dot(spread_weights(joined[DIM:], block), block, preferred_element_type=jnp.float32).astype(jnp.bfloat16)
    return jnp.concatenate([parent_x, parent_up], 0)


def downward_top(sibling, own_x):
    return jnp.dot(sibling[DIM:], kernel_block(sibling[:DIM], own_x), preferred_element_type=jnp.float32).astype(jnp.bfloat16)


def downward_node(sibling, parent_x, parent_down, own_x):
    beside = jnp.dot(sibling[DIM:], kernel_block(sibling[:DIM], own_x), preferred_element_type=jnp.float32)
    above = carry_values(parent_down, kernel_block(parent_x, own_x))
    return (beside + above).astype(jnp.bfloat16)


def near_block(leaves, targets_x, leaf_ids):
    target32 = targets_x.astype(jnp.float32)
    target_norm = jnp.sum(target32 * target32, 1)

    def one_turn(turn, summed):
        source = jnp.take(leaves, leaf_ids[:, turn], axis=0)
        source32 = source[:, :DIM].astype(jnp.float32)
        products = jnp.einsum("bdt,bds->bts", target32, source32, precision=lax.Precision.HIGHEST)
        distance = target_norm[:, :, None] + jnp.sum(source32 * source32, 1)[:, None, :] - 2.0 * products
        weights = jnp.exp(-GAMMA * distance).astype(jnp.bfloat16)
        return summed + jnp.einsum("bts,brs->rbt", weights.astype(jnp.float32), source[:, DIM:].astype(jnp.float32), precision=lax.Precision.HIGHEST)

    start = jnp.zeros((NRHS, targets_x.shape[0], targets_x.shape[2]), jnp.float32)
    return lax.fori_loop(0, leaf_ids.shape[1], one_turn, start)


def reference(points, charges, near_leaves, skel_device, skel_tree):
    nodes = skel_device.shape[0]
    levels = skel_tree.shape[1] + 1
    dev_points = points.shape[1] // nodes
    coords = points.reshape(DIM, nodes, dev_points).transpose(1, 0, 2)
    loads = charges.reshape(NRHS, nodes, dev_points).transpose(1, 0, 2)

    def leaf_up(inputs):
        node_x, node_q, chosen = inputs
        base_x = jnp.take(node_x, chosen, axis=1)
        block = kernel_block(node_x, base_x)
        base_up = jnp.dot(spread_weights(node_q, block), block, preferred_element_type=jnp.float32).astype(jnp.bfloat16)
        return jnp.concatenate([base_x, base_up], 0)

    level_nodes = [lax.map(leaf_up, (coords, loads, skel_device))]
    for height in range(levels - 1):
        current = level_nodes[-1]
        joined = jnp.concatenate([current[0::2], current[1::2]], 2)
        chosen = skel_tree[0::2 ** (height + 1), height]
        level_nodes.append(lax.map(lambda inputs: parent_node(inputs[0], inputs[1]), (joined, chosen)))

    downward = None
    for height in range(levels - 1, -1, -1):
        current = level_nodes[height]
        number = current.shape[0]
        sibling = current.reshape(number // 2, 2, DIM + NRHS, R)[:, ::-1].reshape(number, DIM + NRHS, R)
        if height == levels - 1:
            downward = lax.map(lambda inputs: downward_top(inputs[0], inputs[1][:DIM]), (sibling, current))
        else:
            parent_x = jnp.repeat(level_nodes[height + 1][:, :DIM], 2, axis=0)
            parent_down = jnp.repeat(downward, 2, axis=0)
            downward = lax.map(lambda inputs: downward_node(inputs[0], inputs[1], inputs[2], inputs[3][:DIM]), (sibling, parent_x, parent_down, current))

    base_x = level_nodes[0][:, :DIM]

    def far_field(inputs):
        node_down, node_base, node_x = inputs
        return carry_values(node_down, kernel_block(node_base, node_x))

    far_part = lax.map(far_field, (downward, base_x, coords))

    stacked = jnp.concatenate([points, charges], 0)
    leaves = stacked.reshape(DIM + NRHS, nodes * LEAF_DEV, LEAF).transpose(1, 0, 2)
    id_blocks = near_leaves.reshape(nodes, LEAF_DEV, NNEAR)

    def near_node(inputs):
        node_id, leaf_ids = inputs
        targets = lax.dynamic_slice_in_dim(leaves, (node_id * LEAF_DEV).astype(jnp.int32), LEAF_DEV, 0)
        return near_block(leaves, targets[:, :DIM], leaf_ids).reshape(NRHS, LEAF_DEV * LEAF)

    near_part = lax.map(near_node, (jnp.arange(nodes, dtype=jnp.int32), id_blocks))
    total = near_part + far_part
    return total.transpose(1, 0, 2).reshape(NRHS, nodes * dev_points)
```

```python
import functools

import jax
import jax.numpy as jnp
from jax import lax
from jax.experimental import pallas as pl
from jax.experimental.pallas import tpu as pltpu
from jax.sharding import PartitionSpec as P

DIM = 16
NRHS = 64
DEPTH = 64
GAMMA = 0.125
LOG2E = 1.4426950408889634
MESH = pl.DeviceIdType.MESH
F32 = jnp.float32
BF16 = jnp.bfloat16


def split3(value):
    high = value.astype(BF16).astype(F32)
    rest = value - high
    middle = rest.astype(BF16).astype(F32)
    return [high, middle, rest - middle]


def norms(x32):
    return split3(-(GAMMA * LOG2E) * jnp.sum(x32 * x32, 0, keepdims=True))


def padding(x32):
    return [jnp.zeros((DEPTH - 3 * DIM - 6, x32.shape[1]), F32)]


def row_side(x):
    x32 = x.astype(F32)
    ones = jnp.ones((1, x32.shape[1]), F32)
    parts = split3((2.0 * GAMMA * LOG2E) * x32) + norms(x32) + [ones] * 3 + padding(x32)
    return jnp.concatenate(parts, 0).T.astype(BF16)


def column_side(x):
    x32 = x.astype(F32)
    ones = jnp.ones((1, x32.shape[1]), F32)
    parts = [x32] * 3 + [ones] * 3 + norms(x32) + padding(x32)
    return jnp.concatenate(parts, 0).astype(BF16)


def dot(left, right):
    return jnp.dot(left, right, preferred_element_type=F32)


def dot_nt(left, right):
    return lax.dot_general(left, right, (((1,), (1,)), ((), ())), preferred_element_type=F32)


def gaussian(rows, columns):
    return jnp.exp2(dot(rows, columns)).astype(BF16)


def column_sums(block):
    return jnp.sum(block.astype(F32), 0, keepdims=True)


LANES = 128


def picked(source, chosen):
    depth, blocks = source.shape[0], source.shape[1] // LANES
    stacked = jnp.concatenate([source[:, i * LANES : (i + 1) * LANES] for i in range(blocks)], 0)
    lane, block = chosen & (LANES - 1), chosen >> (LANES.bit_length() - 1)
    index = lax.broadcasted_iota(jnp.int32, (LANES, chosen.shape[1]), 0)
    inside = dot(stacked, jnp.where(index == lane, 1.0, 0.0).astype(BF16))
    total = jnp.zeros((depth, chosen.shape[1]), F32)
    for i in range(blocks):
        total = total + jnp.where(block == i, inside[i * depth : (i + 1) * depth], 0.0)
    return total.astype(BF16)


def kernel(
    inner_levels, outer_levels, near_hbm, x_hbm, q_hbm, device_hbm, tree_hbm, out_ref,
    near_ref, device_ref, tree_ref, x_all, q_all, leaves_q, rows, cols, block0, total0, acc,
    own_x, sib_x, own_u, sib_u, own_blocks, sib_blocks, across_blocks, totals, beside,
    halo_send, halo_recv, x_send, x_recv, u_send, u_recv, local_sem,
):
    inner = 1 << inner_levels
    levels = inner_levels + outer_levels
    outer_id, inner_id = lax.axis_index("outer"), lax.axis_index("inner")
    count = inner << outer_levels
    position = outer_id * inner + inner_id
    n = x_hbm.shape[1]
    leaf_dev, n_near = near_ref.shape
    leaf = n // leaf_dev
    size = device_ref.shape[1]
    has_left, has_right = position > 0, position < count - 1
    left, right = jnp.maximum(position - 1, 0), jnp.minimum(position + 1, count - 1)
    left_id = (left // inner, left % inner)
    right_id = (right // inner, right % inner)

    bits, partners = [], []
    for k in range(levels):
        if k < inner_levels:
            bit = (inner_id // (1 << k)) % 2
            partners.append((outer_id, inner_id + (1 - 2 * bit) * (1 << k)))
        else:
            step = 1 << (k - inner_levels)
            bit = (outer_id // step) % 2
            partners.append((outer_id + (1 - 2 * bit) * step, inner_id))
        bits.append(bit)

    mine = pl.ds(n, n)
    sources = (x_hbm, device_hbm, q_hbm, tree_hbm, near_hbm)
    targets = (x_all.at[:, mine], device_ref, q_all.at[:, mine], tree_ref, near_ref)
    loads = [
        pltpu.make_async_copy(source, target, local_sem.at[i])
        for i, (source, target) in enumerate(zip(sources, targets))
    ]
    for load in loads:
        load.start()

    barrier = pltpu.get_barrier_semaphore()
    for peer in partners:
        pl.semaphore_signal(barrier, inc=1, device_id=peer, device_id_type=MESH)

    @pl.when(has_left)
    def _():
        pl.semaphore_signal(barrier, inc=1, device_id=left_id, device_id_type=MESH)

    @pl.when(has_right)
    def _():
        pl.semaphore_signal(barrier, inc=1, device_id=right_id, device_id_type=MESH)

    def halo(source, target, which, peer):
        return pltpu.make_async_remote_copy(
            src_ref=source, dst_ref=target, send_sem=halo_send.at[which],
            recv_sem=halo_recv.at[which], device_id=peer, device_id_type=MESH,
        )

    first, last = pl.ds(0, n), pl.ds(2 * n, n)
    rightward = [
        halo(x_hbm, x_all.at[:, first], 0, right_id),
        halo(q_hbm, q_all.at[:, first], 1, right_id),
    ]
    leftward = [
        halo(x_hbm, x_all.at[:, last], 2, left_id),
        halo(q_hbm, q_all.at[:, last], 3, left_id),
    ]

    def exchange(source, target, send, recv, k):
        return pltpu.make_async_remote_copy(
            src_ref=source.at[k], dst_ref=target.at[k], send_sem=send.at[k],
            recv_sem=recv.at[k], device_id=partners[k], device_id_type=MESH,
        )

    send_x = [exchange(own_x, sib_x, x_send, x_recv, k) for k in range(levels)]
    send_u = [exchange(own_u, sib_u, u_send, u_recv, k) for k in range(levels)]

    loads[0].wait()
    loads[1].wait()
    base_x = picked(x_all[:, mine], device_ref[...])
    own_x[0] = base_x

    beside_us = (position + count - 1) // count + 1 - (position + 1) // count
    pl.semaphore_wait(barrier, levels + beside_us)
    send_x[0].start()

    @pl.when(has_right)
    def _():
        for copy in rightward:
            copy.start()

    @pl.when(has_left)
    def _():
        for copy in leftward:
            copy.start()

    def columns_of(j, _):
        source = pl.ds(pl.multiple_of(n + j * leaf, leaf), leaf)
        part = pl.ds(pl.multiple_of(j * leaf, leaf), leaf)
        cols[:, part] = column_side(x_all[:, source])
        return 0

    lax.fori_loop(0, leaf_dev, columns_of, 0, unroll=4)

    def prepare(start):
        def one(j, _):
            part = pl.ds(pl.multiple_of((start + j) * leaf, leaf), leaf)
            rows[start + j] = row_side(x_all[:, part])
            leaves_q[start + j] = q_all[:, part]
            return 0

        lax.fori_loop(0, leaf_dev, one, 0, unroll=8)

    chunk = 512
    wide = n // chunk
    base_rows = row_side(base_x)
    acc[...] = jnp.zeros_like(acc)

    def base(c, _):
        part = pl.ds(pl.multiple_of(c * chunk, chunk), chunk)
        source = pl.ds(pl.multiple_of(n + c * chunk, chunk), chunk)
        block = gaussian(base_rows, cols[:, part])
        inverse = 1.0 / column_sums(block)
        block0[:, part] = block
        total0[:, part] = inverse
        weights = (q_all[:, source].astype(F32) * inverse).astype(BF16)
        acc[...] += dot_nt(weights, block)
        return 0

    for load in loads[2:]:
        load.wait()
    lax.fori_loop(0, wide, base, 0, unroll=2)
    own_u[0] = acc[...].astype(BF16)
    send_u[0].start()

    def coordinates(k):
        send_x[k].wait_recv()
        own, sib = own_x[k], sib_x[k]
        own_cols = column_side(own)
        if k < levels - 1:
            shifted = tree_ref[0, k : k + 1, :] + bits[k] * size
            chosen = jnp.where(shifted >= 2 * size, shifted - 2 * size, shifted)
            parent = picked(jnp.concatenate([own, sib], 1), chosen)
            own_x[k + 1] = parent
            send_x[k + 1].start()
            parent_rows = row_side(parent)
            for which, columns, kept in ((0, own_cols, own_blocks), (1, column_side(sib), sib_blocks)):
                block = gaussian(parent_rows, columns)
                kept[k] = block
                totals[2 * k + which : 2 * k + which + 1, :] = 1.0 / column_sums(block)
        across_blocks[k] = gaussian(row_side(sib), own_cols)

    def raised(values, k, which, blocks):
        inverse = totals[2 * k + which : 2 * k + which + 1, :]
        return dot_nt((values.astype(F32) * inverse).astype(BF16), blocks[k])

    def charges(k, part):
        send_u[k].wait_recv()
        if k < levels - 1:
            own_u[k + 1] = (part + raised(sib_u[k], k, 1, sib_blocks)).astype(BF16)
            send_u[k + 1].start()
        beside[k] = dot(sib_u[k], across_blocks[k])

    def near_sum(b):
        part = pl.ds(pl.multiple_of(b * leaf, leaf), leaf)
        columns = cols[:, part]
        weights, sides = [], []
        for turn in range(n_near):
            number = near_ref[b, turn] - (position - 1) * leaf_dev
            number = jnp.minimum(jnp.maximum(number, 0), 3 * leaf_dev - 1)
            weights.append(gaussian(rows[number], columns))
            sides.append(leaves_q[number])
        return part, dot(jnp.concatenate(sides, 1), jnp.concatenate(weights, 0))

    def near(b, _):
        part, value = near_sum(b)
        out_ref[:, part] = value
        return 0

    def halos():
        @pl.when(has_left)
        def _():
            for copy in rightward:
                copy.wait_recv()

        @pl.when(has_right)
        def _():
            for copy in leftward:
                copy.wait_recv()

        prepare(0)
        prepare(2 * leaf_dev)

    first_near, share = 2, 2

    done = 0
    coordinates(0)
    prepare(leaf_dev)
    for k in range(levels):
        if k < levels - 1:
            coordinates(k + 1)
            part = raised(own_u[k], k, 0, own_blocks)
        if k == min(first_near, levels - 1):
            halos()
        if k >= first_near:
            ahead = min(leaf_dev, done + share)
            lax.fori_loop(done, ahead, near, 0)
            done = ahead
        charges(k, part)

    down = beside[levels - 1].astype(BF16)
    for k in range(levels - 2, -1, -1):
        down = (beside[k] + dot(down, own_blocks[k]) * totals[2 * k : 2 * k + 1, :]).astype(BF16)

    def far(b, _):
        part = pl.ds(pl.multiple_of(b * leaf, leaf), leaf)
        out_ref[:, part] += dot(down, block0[:, part]) * total0[:, part]
        return 0

    def both(b, _):
        part, value = near_sum(b)
        out_ref[:, part] = value + dot(down, block0[:, part]) * total0[:, part]
        return 0

    if done > 0:
        lax.fori_loop(0, done, far, 0, unroll=2)
    if done < leaf_dev:
        lax.fori_loop(done, leaf_dev, both, 0)

    for copy in send_x + send_u:
        copy.wait_send()

    @pl.when(has_right)
    def _():
        for copy in rightward:
            copy.wait_send()

    @pl.when(has_left)
    def _():
        for copy in leftward:
            copy.wait_send()


def body(points, charges, near_leaves, skel_device, skel_tree):
    inner_levels = lax.axis_size("inner").bit_length() - 1
    outer_levels = lax.axis_size("outer").bit_length() - 1
    levels = inner_levels + outer_levels
    n, size = points.shape[1], skel_device.shape[1]
    leaf_dev = near_leaves.shape[0]
    leaf = n // leaf_dev
    coordinates = pltpu.VMEM((levels, DIM, size), BF16)
    loads = pltpu.VMEM((levels, NRHS, size), BF16)
    blocks = pltpu.VMEM((levels, size, size), BF16)
    each = pltpu.SemaphoreType.DMA((levels,))
    return pl.pallas_call(
        functools.partial(kernel, inner_levels, outer_levels),
        out_shape=jax.ShapeDtypeStruct((NRHS, n), F32),
        in_specs=[pl.BlockSpec(memory_space=pltpu.HBM)] * 5,
        out_specs=pl.BlockSpec(memory_space=pltpu.VMEM),
        scratch_shapes=[
            pltpu.SMEM(near_leaves.shape, jnp.int32),
            pltpu.VMEM(skel_device.shape, jnp.int32),
            pltpu.VMEM(skel_tree.shape, jnp.int32),
            pltpu.VMEM((DIM, 3 * n), BF16),
            pltpu.VMEM((NRHS, 3 * n), BF16),
            pltpu.VMEM((3 * leaf_dev, NRHS, leaf), BF16),
            pltpu.VMEM((3 * leaf_dev, leaf, DEPTH), BF16),
            pltpu.VMEM((DEPTH, n), BF16),
            pltpu.VMEM((size, n), BF16),
            pltpu.VMEM((1, n), F32),
            pltpu.VMEM((NRHS, size), F32),
            coordinates, coordinates, loads, loads, blocks, blocks, blocks,
            pltpu.VMEM((2 * levels, size), F32),
            pltpu.VMEM((levels, NRHS, size), F32),
            pltpu.SemaphoreType.DMA((4,)),
            pltpu.SemaphoreType.DMA((4,)),
            each, each, each, each,
            pltpu.SemaphoreType.DMA((5,)),
        ],
        compiler_params=pltpu.CompilerParams(
            collective_id=0, has_side_effects=True, vmem_limit_bytes=60 << 20
        ),
        name="skeleton_matvec",
    )(near_leaves, points, charges, skel_device, skel_tree)


def solution(mesh):
    return jax.shard_map(
        body,
        mesh=mesh,
        in_specs=(
            P(None, ("outer", "inner")),
            P(None, ("outer", "inner")),
            P(("outer", "inner"), None),
            P(("outer", "inner"), None),
            P(("outer", "inner"), None, None),
        ),
        out_specs=P(None, ("outer", "inner")),
        check_vma=False,
    )
```

```python
import functools

import jax
import jax.numpy as jnp
from jax import lax
from jax.experimental import pallas as pl
from jax.experimental.pallas import tpu as pltpu
from jax.sharding import PartitionSpec as P

DIM = 16
NRHS = 64
DEPTH = 64
GAMMA = 0.125
LOG2E = 1.4426950408889634
MESH = pl.DeviceIdType.MESH
F32 = jnp.float32
BF16 = jnp.bfloat16


def split3(value):
    high = value.astype(BF16).astype(F32)
    rest = value - high
    middle = rest.astype(BF16).astype(F32)
    return [high, middle, rest - middle]


def norms(x32):
    return split3(-(GAMMA * LOG2E) * jnp.sum(x32 * x32, 0, keepdims=True))


def padding(x32):
    return [jnp.zeros((DEPTH - 3 * DIM - 6, x32.shape[1]), F32)]


def row_side(x):
    x32 = x.astype(F32)
    ones = jnp.ones((1, x32.shape[1]), F32)
    parts = split3((2.0 * GAMMA * LOG2E) * x32) + norms(x32) + [ones] * 3 + padding(x32)
    return jnp.concatenate(parts, 0).T.astype(BF16)


def column_side(x):
    x32 = x.astype(F32)
    ones = jnp.ones((1, x32.shape[1]), F32)
    parts = [x32] * 3 + [ones] * 3 + norms(x32) + padding(x32)
    return jnp.concatenate(parts, 0).astype(BF16)


def dot(left, right):
    return jnp.dot(left, right, preferred_element_type=F32)


def dot_nt(left, right):
    return lax.dot_general(left, right, (((1,), (1,)), ((), ())), preferred_element_type=F32)


def gaussian(rows, columns):
    return jnp.exp2(dot(rows, columns)).astype(BF16)


def column_sums(block):
    return jnp.sum(block.astype(F32), 0, keepdims=True)


LANES = 128


def picked(source, chosen):
    depth, blocks = source.shape[0], source.shape[1] // LANES
    stacked = jnp.concatenate([source[:, i * LANES : (i + 1) * LANES] for i in range(blocks)], 0)
    lane, block = chosen & (LANES - 1), chosen >> (LANES.bit_length() - 1)
    index = lax.broadcasted_iota(jnp.int32, (LANES, chosen.shape[1]), 0)
    inside = dot(stacked, jnp.where(index == lane, 1.0, 0.0).astype(BF16))
    total = jnp.zeros((depth, chosen.shape[1]), F32)
    for i in range(blocks):
        total = total + jnp.where(block == i, inside[i * depth : (i + 1) * depth], 0.0)
    return total.astype(BF16)


def kernel(
    inner_levels, outer_levels, near_hbm, x_hbm, q_hbm, device_hbm, tree_hbm, out_ref,
    near_ref, device_ref, tree_ref, x_all, q_ref, leaves_q, rows, cols, block0, total0, acc,
    own_x, sib_x, own_u, sib_u, own_blocks, sib_block, across_blocks, totals, beside, kept,
    halo_send, halo_recv, piece_send, piece_recv, x_send, x_recv, u_send, u_recv, local_sem,
):
    inner = 1 << inner_levels
    levels = inner_levels + outer_levels
    outer_id, inner_id = lax.axis_index("outer"), lax.axis_index("inner")
    count = inner << outer_levels
    position = outer_id * inner + inner_id
    n = x_hbm.shape[1]
    leaf_dev, n_near = near_ref.shape
    leaf = n // leaf_dev
    size = device_ref.shape[1]
    has_left, has_right = position > 0, position < count - 1
    left, right = jnp.maximum(position - 1, 0), jnp.minimum(position + 1, count - 1)
    left_id = (left // inner, left % inner)
    right_id = (right // inner, right % inner)

    def partner(step):
        bit = (position // step) % 2
        other = position + (1 - 2 * bit) * step
        return bit, (other // inner, other % inner)

    mine = pl.ds(n, n)
    sources = (x_hbm, device_hbm, q_hbm, tree_hbm, near_hbm)
    targets = (x_all.at[:, mine], device_ref, q_ref, tree_ref, near_ref)
    loads = [
        pltpu.make_async_copy(source, target, local_sem.at[i])
        for i, (source, target) in enumerate(zip(sources, targets))
    ]
    for load in loads:
        load.start()

    barrier = pltpu.get_barrier_semaphore()
    for k in range(levels):
        pl.semaphore_signal(barrier, inc=1, device_id=partner(1 << k)[1], device_id_type=MESH)

    @pl.when(has_left)
    def _():
        pl.semaphore_signal(barrier, inc=1, device_id=left_id, device_id_type=MESH)

    @pl.when(has_right)
    def _():
        pl.semaphore_signal(barrier, inc=1, device_id=right_id, device_id_type=MESH)

    def halo(source, target, send, recv, peer):
        return pltpu.make_async_remote_copy(
            src_ref=source, dst_ref=target, send_sem=send, recv_sem=recv,
            device_id=peer, device_id_type=MESH,
        )

    first, last = pl.ds(0, n), pl.ds(2 * n, n)
    rightward = halo(x_hbm, x_all.at[:, first], halo_send.at[0], halo_recv.at[0], right_id)
    leftward = halo(x_hbm, x_all.at[:, last], halo_send.at[1], halo_recv.at[1], left_id)

    def piece(j, side):
        part = pl.ds(pl.multiple_of(j * leaf, leaf), leaf)
        return halo(
            q_hbm.at[:, part], leaves_q.at[2 * side * leaf_dev + j], piece_send.at[side, j],
            piece_recv.at[side, j], (right_id, left_id)[side],
        )

    def feed(j):
        @pl.when(has_right)
        def _():
            piece(j, 0).start()

        @pl.when(has_left)
        def _():
            piece(j, 1).start()

    def exchange(source, target, send, recv, k, peer):
        return pltpu.make_async_remote_copy(
            src_ref=source.at[k], dst_ref=target.at[k], send_sem=send.at[k],
            recv_sem=recv.at[k], device_id=peer, device_id_type=MESH,
        )

    def send_x(k, peer):
        return exchange(own_x, sib_x, x_send, x_recv, k, peer)

    def send_u(k, peer):
        return exchange(own_u, sib_u, u_send, u_recv, k, peer)

    loads[0].wait()
    loads[1].wait()
    base_x = picked(x_all[:, mine], device_ref[...])
    own_x[0] = base_x

    beside_us = (position + count - 1) // count + 1 - (position + 1) // count
    pl.semaphore_wait(barrier, levels + beside_us)
    send_x(0, partner(1)[1]).start()

    @pl.when(has_right)
    def _():
        rightward.start()

    @pl.when(has_left)
    def _():
        leftward.start()

    def columns_of(j, _):
        source = pl.ds(pl.multiple_of(n + j * leaf, leaf), leaf)
        part = pl.ds(pl.multiple_of(j * leaf, leaf), leaf)
        cols[:, part] = column_side(x_all[:, source])
        return 0

    lax.fori_loop(0, leaf_dev, columns_of, 0, unroll=4)

    def prepare(start):
        def one(j, _):
            part = pl.ds(pl.multiple_of((start + j) * leaf, leaf), leaf)
            rows[start + j] = row_side(x_all[:, part])
            return 0

        lax.fori_loop(0, leaf_dev, one, 0, unroll=4)

    chunk = 512
    wide = n // chunk
    base_rows = row_side(base_x)
    acc[...] = jnp.zeros_like(acc)

    def base(pair, _):
        feed(pair)
        for c in (2 * pair, 2 * pair + 1):
            part = pl.ds(pl.multiple_of(c * chunk, chunk), chunk)
            block = gaussian(base_rows, cols[:, part])
            inverse = 1.0 / column_sums(block)
            block0[:, part] = block
            total0[:, part] = inverse
            weights = (q_ref[:, part].astype(F32) * inverse).astype(BF16)
            acc[...] += dot_nt(weights, block)
        return 0

    for load in loads[2:]:
        load.wait()
    lax.fori_loop(0, wide // 2, base, 0)
    own_u[0] = acc[...].astype(BF16)
    send_u(0, partner(1)[1]).start()
    fed = wide // 2

    def tree_blocks(k, bit, peer_above):
        own, sib = own_x[k], sib_x[k]
        own_cols = column_side(own)
        shifted = tree_ref[0, pl.ds(k, 1), :] + bit * size
        chosen = jnp.where(shifted >= 2 * size, shifted - 2 * size, shifted)
        parent = picked(jnp.concatenate([own, sib], 1), chosen)
        own_x[k + 1] = parent
        send_x(k + 1, peer_above).start()
        parent_rows = row_side(parent)
        block = gaussian(parent_rows, own_cols)
        own_blocks[k] = block
        totals[k, 0:1, :] = 1.0 / column_sums(block)
        block = gaussian(parent_rows, column_side(sib))
        sib_block[k] = block
        totals[k, 1:2, :] = 1.0 / column_sums(block)

    def across(k):
        across_blocks[k] = gaussian(row_side(sib_x[k]), column_side(own_x[k]))

    def raised(values, k, which, blocks):
        return dot_nt((values.astype(F32) * totals[k, which : which + 1, :]).astype(BF16), blocks[k])

    def number_of(b, turn):
        number = near_ref[b, turn] - (position - 1) * leaf_dev
        return jnp.minimum(jnp.maximum(number, 0), 3 * leaf_dev - 1)

    def near_weights(b, _):
        feed(ahead + b)
        columns = cols[:, pl.ds(pl.multiple_of(b * leaf, leaf), leaf)]
        for turn in range(n_near):
            kept[b, turn * leaf : (turn + 1) * leaf, :] = gaussian(rows[number_of(b, turn)], columns)
        return 0

    send_x(0, partner(1)[1]).wait_recv()
    feed(fed)
    tree_blocks(0, partner(1)[0], partner(2)[1])
    across(0)
    feed(fed + 1)

    def own_leaves(j, _):
        part = pl.ds(pl.multiple_of(j * leaf, leaf), leaf)
        leaves_q[leaf_dev + j] = q_ref[:, part]
        return 0

    lax.fori_loop(0, leaf_dev, own_leaves, 0, unroll=4)
    prepare(leaf_dev)

    @pl.when(has_left)
    def _():
        rightward.wait_recv()

    feed(fed + 2)
    prepare(0)

    @pl.when(has_right)
    def _():
        leftward.wait_recv()

    feed(fed + 3)
    prepare(2 * leaf_dev)
    ahead = fed + 4
    share = kept.shape[0] // (levels - 1)

    def level(k, step):
        _, peer = partner(step)
        bit, peer_above = partner(2 * step)
        send_x(k + 1, peer_above).wait_recv()

        @pl.when(k < levels - 2)
        def _():
            tree_blocks(k + 1, bit, partner(jnp.minimum(4 * step, count // 2))[1])

        across(k + 1)
        part = raised(own_u[k], k, 0, own_blocks)
        lax.fori_loop(k * share, (k + 1) * share, near_weights, 0)
        send_u(k, peer).wait_recv()
        own_u[k + 1] = (part + raised(sib_u[k], k, 1, sib_block)).astype(BF16)
        send_u(k + 1, peer_above).start()
        beside[k] = dot(sib_u[k], across_blocks[k])
        return 2 * step

    lax.fori_loop(0, levels - 1, level, jnp.int32(1))
    done = (levels - 1) * share
    for j in range(ahead + done, leaf_dev):
        feed(j)

    def arrived(j, _):
        @pl.when(has_left)
        def _():
            piece(j, 0).wait_recv()

        @pl.when(has_right)
        def _():
            piece(j, 1).wait_recv()

        return 0

    lax.fori_loop(0, leaf_dev, arrived, 0)

    def near_sum(b, _):
        part = pl.ds(pl.multiple_of(b * leaf, leaf), leaf)
        sides = [leaves_q[number_of(b, turn)] for turn in range(n_near)]
        out_ref[:, part] = dot(jnp.concatenate(sides, 1), kept[b])
        return 0

    lax.fori_loop(0, done, near_sum, 0)

    top = levels - 1
    send_u(top, partner(1 << top)[1]).wait_recv()
    down = dot(sib_u[top], across_blocks[top]).astype(BF16)
    for k in range(levels - 2, -1, -1):
        down = (beside[k] + dot(down, own_blocks[k]) * totals[k, 0:1, :]).astype(BF16)

    def far(b, _):
        part = pl.ds(pl.multiple_of(b * leaf, leaf), leaf)
        out_ref[:, part] += dot(down, block0[:, part]) * total0[:, part]
        return 0

    def both(b, _):
        part = pl.ds(pl.multiple_of(b * leaf, leaf), leaf)
        columns = cols[:, part]
        weights, sides = [], []
        for turn in range(n_near):
            number = number_of(b, turn)
            weights.append(gaussian(rows[number], columns))
            sides.append(leaves_q[number])
        value = dot(jnp.concatenate(sides, 1), jnp.concatenate(weights, 0))
        out_ref[:, part] = value + dot(down, block0[:, part]) * total0[:, part]
        return 0

    lax.fori_loop(0, done, far, 0, unroll=2)
    lax.fori_loop(done, leaf_dev, both, 0)

    for k in range(levels):
        peer = partner(1 << k)[1]
        send_x(k, peer).wait_send()
        send_u(k, peer).wait_send()

    def sent(j, _):
        @pl.when(has_right)
        def _():
            piece(j, 0).wait_send()

        @pl.when(has_left)
        def _():
            piece(j, 1).wait_send()

        return 0

    lax.fori_loop(0, leaf_dev, sent, 0)

    @pl.when(has_right)
    def _():
        rightward.wait_send()

    @pl.when(has_left)
    def _():
        leftward.wait_send()


def body(points, charges, near_leaves, skel_device, skel_tree):
    inner_levels = lax.axis_size("inner").bit_length() - 1
    outer_levels = lax.axis_size("outer").bit_length() - 1
    levels = inner_levels + outer_levels
    n, size = points.shape[1], skel_device.shape[1]
    leaf_dev = near_leaves.shape[0]
    leaf = n // leaf_dev
    coordinates = pltpu.VMEM((levels, DIM, size), BF16)
    loads = pltpu.VMEM((levels, NRHS, size), BF16)
    blocks = pltpu.VMEM((levels, size, size), BF16)
    each = pltpu.SemaphoreType.DMA((levels,))
    return pl.pallas_call(
        functools.partial(kernel, inner_levels, outer_levels),
        out_shape=jax.ShapeDtypeStruct((NRHS, n), F32),
        in_specs=[pl.BlockSpec(memory_space=pltpu.HBM)] * 5,
        out_specs=pl.BlockSpec(memory_space=pltpu.VMEM),
        scratch_shapes=[
            pltpu.SMEM(near_leaves.shape, jnp.int32),
            pltpu.VMEM(skel_device.shape, jnp.int32),
            pltpu.VMEM(skel_tree.shape, jnp.int32),
            pltpu.VMEM((DIM, 3 * n), BF16),
            pltpu.VMEM(charges.shape, BF16),
            pltpu.VMEM((3 * leaf_dev, NRHS, leaf), BF16),
            pltpu.VMEM((3 * leaf_dev, leaf, DEPTH), BF16),
            pltpu.VMEM((DEPTH, n), BF16),
            pltpu.VMEM((size, n), BF16),
            pltpu.VMEM((1, n), F32),
            pltpu.VMEM((NRHS, size), F32),
            coordinates, coordinates, loads, loads, blocks, blocks, blocks,
            pltpu.VMEM((levels, 2, size), F32),
            pltpu.VMEM((levels, NRHS, size), F32),
            pltpu.VMEM((leaf_dev // 2, near_leaves.shape[1] * leaf, leaf), BF16),
            pltpu.SemaphoreType.DMA((2,)),
            pltpu.SemaphoreType.DMA((2,)),
            pltpu.SemaphoreType.DMA((2, leaf_dev)),
            pltpu.SemaphoreType.DMA((2, leaf_dev)),
            each, each, each, each,
            pltpu.SemaphoreType.DMA((5,)),
        ],
        compiler_params=pltpu.CompilerParams(
            collective_id=0, has_side_effects=True, vmem_limit_bytes=58 << 20
        ),
        name="skeleton_matvec",
    )(near_leaves, points, charges, skel_device, skel_tree)


def solution(mesh):
    return jax.shard_map(
        body,
        mesh=mesh,
        in_specs=(
            P(None, ("outer", "inner")),
            P(None, ("outer", "inner")),
            P(("outer", "inner"), None),
            P(("outer", "inner"), None),
            P(("outer", "inner"), None, None),
        ),
        out_specs=P(None, ("outer", "inner")),
        check_vma=False,
    )
```

```python
import functools

import jax
import jax.numpy as jnp
from jax import lax
from jax.experimental import pallas as pl
from jax.experimental.pallas import tpu as pltpu
from jax.sharding import PartitionSpec as P

DIM = 16
NRHS = 64
DEPTH = 64
GAMMA = 0.125
LOG2E = 1.4426950408889634
MESH = pl.DeviceIdType.MESH
F32 = jnp.float32
BF16 = jnp.bfloat16


def split3(value):
    high = value.astype(BF16).astype(F32)
    rest = value - high
    middle = rest.astype(BF16).astype(F32)
    return [high, middle, rest - middle]


def norms(x32):
    return split3(-(GAMMA * LOG2E) * jnp.sum(x32 * x32, 0, keepdims=True))


def padding(x32):
    return [jnp.zeros((DEPTH - 3 * DIM - 6, x32.shape[1]), F32)]


def row_side(x):
    x32 = x.astype(F32)
    ones = jnp.ones((1, x32.shape[1]), F32)
    parts = split3((2.0 * GAMMA * LOG2E) * x32) + norms(x32) + [ones] * 3 + padding(x32)
    return jnp.concatenate(parts, 0).T.astype(BF16)


def column_side(x):
    x32 = x.astype(F32)
    ones = jnp.ones((1, x32.shape[1]), F32)
    parts = [x32] * 3 + [ones] * 3 + norms(x32) + padding(x32)
    return jnp.concatenate(parts, 0).astype(BF16)


def dot(left, right):
    return jnp.dot(left, right, preferred_element_type=F32)


def dot_nt(left, right):
    return lax.dot_general(left, right, (((1,), (1,)), ((), ())), preferred_element_type=F32)


def gaussian(rows, columns):
    return jnp.exp2(dot(rows, columns)).astype(BF16)


def column_sums(block):
    return jnp.sum(block.astype(F32), 0, keepdims=True)


LANES = 128


def picked(source, chosen):
    depth, blocks = source.shape[0], source.shape[1] // LANES
    stacked = jnp.concatenate([source[:, i * LANES : (i + 1) * LANES] for i in range(blocks)], 0)
    lane, block = chosen & (LANES - 1), chosen >> (LANES.bit_length() - 1)
    index = lax.broadcasted_iota(jnp.int32, (LANES, chosen.shape[1]), 0)
    inside = dot(stacked, jnp.where(index == lane, 1.0, 0.0).astype(BF16))
    total = jnp.zeros((depth, chosen.shape[1]), F32)
    for i in range(blocks):
        total = total + jnp.where(block == i, inside[i * depth : (i + 1) * depth], 0.0)
    return total.astype(BF16)


def kernel(
    inner_levels, outer_levels, near_hbm, x_hbm, q_hbm, device_hbm, tree_hbm, out_ref,
    near_ref, device_ref, tree_ref, x_all, q_ref, leaves_q, rows, cols, block0, total0, acc,
    own_x, sib_x, own_u, sib_u, own_blocks, sib_block, across_blocks, totals, beside, kept,
    halo_send, halo_recv, piece_send, piece_recv, x_send, x_recv, u_send, u_recv, local_sem,
):
    inner = 1 << inner_levels
    levels = inner_levels + outer_levels
    outer_id, inner_id = lax.axis_index("outer"), lax.axis_index("inner")
    count = inner << outer_levels
    position = outer_id * inner + inner_id
    n = x_hbm.shape[1]
    leaf_dev, n_near = near_ref.shape
    leaf = n // leaf_dev
    size = device_ref.shape[1]
    has_left, has_right = position > 0, position < count - 1
    left, right = jnp.maximum(position - 1, 0), jnp.minimum(position + 1, count - 1)
    left_id = (left // inner, left % inner)
    right_id = (right // inner, right % inner)

    def partner(step):
        bit = (position // step) % 2
        other = position + (1 - 2 * bit) * step
        return bit, (other // inner, other % inner)

    mine = pl.ds(n, n)
    sources = (x_hbm, device_hbm, q_hbm, tree_hbm, near_hbm)
    targets = (x_all.at[:, mine], device_ref, q_ref, tree_ref, near_ref)
    loads = [
        pltpu.make_async_copy(source, target, local_sem.at[i])
        for i, (source, target) in enumerate(zip(sources, targets))
    ]
    for load in loads:
        load.start()

    barrier = pltpu.get_barrier_semaphore()
    for k in range(levels):
        pl.semaphore_signal(barrier, inc=1, device_id=partner(1 << k)[1], device_id_type=MESH)

    @pl.when(has_left)
    def _():
        pl.semaphore_signal(barrier, inc=1, device_id=left_id, device_id_type=MESH)

    @pl.when(has_right)
    def _():
        pl.semaphore_signal(barrier, inc=1, device_id=right_id, device_id_type=MESH)

    def halo(source, target, send, recv, peer):
        return pltpu.make_async_remote_copy(
            src_ref=source, dst_ref=target, send_sem=send, recv_sem=recv,
            device_id=peer, device_id_type=MESH,
        )

    first, last = pl.ds(0, n), pl.ds(2 * n, n)
    rightward = halo(x_hbm, x_all.at[:, first], halo_send.at[0], halo_recv.at[0], right_id)
    leftward = halo(x_hbm, x_all.at[:, last], halo_send.at[1], halo_recv.at[1], left_id)

    def piece(j, side):
        part = pl.ds(pl.multiple_of(j * leaf, leaf), leaf)
        return halo(
            q_hbm.at[:, part], leaves_q.at[2 * side * leaf_dev + j], piece_send.at[side, j],
            piece_recv.at[side, j], (right_id, left_id)[side],
        )

    def feed(j):
        @pl.when(has_right)
        def _():
            piece(j, 0).start()

        @pl.when(has_left)
        def _():
            piece(j, 1).start()

    def exchange(source, target, send, recv, k, peer):
        return pltpu.make_async_remote_copy(
            src_ref=source.at[k], dst_ref=target.at[k], send_sem=send.at[k],
            recv_sem=recv.at[k], device_id=peer, device_id_type=MESH,
        )

    def send_x(k, peer):
        return exchange(own_x, sib_x, x_send, x_recv, k, peer)

    def send_u(k, peer):
        return exchange(own_u, sib_u, u_send, u_recv, k, peer)

    loads[0].wait()
    loads[1].wait()
    base_x = picked(x_all[:, mine], device_ref[...])
    own_x[0] = base_x

    def columns_of(j, _):
        source = pl.ds(pl.multiple_of(n + j * leaf, leaf), leaf)
        part = pl.ds(pl.multiple_of(j * leaf, leaf), leaf)
        cols[:, part] = column_side(x_all[:, source])
        return 0

    lax.fori_loop(0, leaf_dev, columns_of, 0, unroll=4)

    def prepare(start):
        def one(j, _):
            part = pl.ds(pl.multiple_of((start + j) * leaf, leaf), leaf)
            rows[start + j] = row_side(x_all[:, part])
            return 0

        lax.fori_loop(0, leaf_dev, one, 0, unroll=4)

    def own_leaves(j, _):
        part = pl.ds(pl.multiple_of(j * leaf, leaf), leaf)
        leaves_q[leaf_dev + j] = q_ref[:, part]
        return 0

    loads[2].wait()
    lax.fori_loop(0, leaf_dev, own_leaves, 0, unroll=4)
    prepare(leaf_dev)

    beside_us = (position + count - 1) // count + 1 - (position + 1) // count
    pl.semaphore_wait(barrier, levels + beside_us)
    send_x(0, partner(1)[1]).start()

    @pl.when(has_right)
    def _():
        rightward.start()

    @pl.when(has_left)
    def _():
        leftward.start()

    chunk = 512
    wide = n // chunk
    base_rows = row_side(base_x)
    acc[...] = jnp.zeros_like(acc)

    def base(pair, _):
        for c in (2 * pair, 2 * pair + 1):
            part = pl.ds(pl.multiple_of(c * chunk, chunk), chunk)
            block = gaussian(base_rows, cols[:, part])
            inverse = 1.0 / column_sums(block)
            block0[:, part] = block
            total0[:, part] = inverse
            weights = (q_ref[:, part].astype(F32) * inverse).astype(BF16)
            acc[...] += dot_nt(weights, block)
        return 0

    for load in loads[3:]:
        load.wait()
    lax.fori_loop(0, wide // 2, base, 0)
    own_u[0] = acc[...].astype(BF16)
    send_u(0, partner(1)[1]).start()
    fed = 0

    def tree_blocks(k, bit, peer_above):
        own, sib = own_x[k], sib_x[k]
        own_cols = column_side(own)
        shifted = tree_ref[0, pl.ds(k, 1), :] + bit * size
        chosen = jnp.where(shifted >= 2 * size, shifted - 2 * size, shifted)
        parent = picked(jnp.concatenate([own, sib], 1), chosen)
        own_x[k + 1] = parent
        send_x(k + 1, peer_above).start()
        parent_rows = row_side(parent)
        block = gaussian(parent_rows, own_cols)
        own_blocks[k] = block
        totals[k, 0:1, :] = 1.0 / column_sums(block)
        block = gaussian(parent_rows, column_side(sib))
        sib_block[k % 2] = block
        totals[k, 1:2, :] = 1.0 / column_sums(block)

    def across(k):
        across_blocks[k % 2] = gaussian(row_side(sib_x[k]), column_side(own_x[k]))

    def raised(values, k, which, block):
        return dot_nt((values.astype(F32) * totals[k, which : which + 1, :]).astype(BF16), block)

    def number_of(b, turn):
        number = near_ref[b, turn] - (position - 1) * leaf_dev
        return jnp.minimum(jnp.maximum(number, 0), 3 * leaf_dev - 1)

    def near_weights(b, _):
        @pl.when(ahead + b < leaf_dev)
        def _():
            feed(ahead + b)

        columns = cols[:, pl.ds(pl.multiple_of(b * leaf, leaf), leaf)]
        for turn in range(n_near):
            kept[b, turn * leaf : (turn + 1) * leaf, :] = gaussian(rows[number_of(b, turn)], columns)
        return 0

    send_x(0, partner(1)[1]).wait_recv()
    feed(fed)
    tree_blocks(0, partner(1)[0], partner(2)[1])
    across(0)
    feed(fed + 1)

    @pl.when(has_left)
    def _():
        rightward.wait_recv()

    feed(fed + 2)
    prepare(0)

    @pl.when(has_right)
    def _():
        leftward.wait_recv()

    feed(fed + 3)
    prepare(2 * leaf_dev)
    ahead = fed + 4
    share = max(1, 4 * 4 // (levels - 1))

    def level(k, step):
        _, peer = partner(step)
        bit, peer_above = partner(2 * step)
        lax.fori_loop(k * share, (k + 1) * share, near_weights, 0)
        send_x(k + 1, peer_above).wait_recv()

        @pl.when(k < levels - 2)
        def _():
            tree_blocks(k + 1, bit, partner(jnp.minimum(4 * step, count // 2))[1])

        across(k + 1)
        part = raised(own_u[k], k, 0, own_blocks[k])
        send_u(k, peer).wait_recv()
        own_u[k + 1] = (part + raised(sib_u[k], k, 1, sib_block[k % 2])).astype(BF16)
        send_u(k + 1, peer_above).start()
        beside[k] = dot(sib_u[k], across_blocks[k % 2])
        return 2 * step

    lax.fori_loop(0, levels - 1, level, jnp.int32(1))
    done = (levels - 1) * share
    if done < leaf_dev:
        lax.fori_loop(done, leaf_dev, near_weights, 0)

    def arrived(j, _):
        @pl.when(has_left)
        def _():
            piece(j, 0).wait_recv()

        @pl.when(has_right)
        def _():
            piece(j, 1).wait_recv()

        return 0

    lax.fori_loop(0, leaf_dev, arrived, 0)

    def near_sum(b, _):
        part = pl.ds(pl.multiple_of(b * leaf, leaf), leaf)
        sides = [leaves_q[number_of(b, turn)] for turn in range(n_near)]
        out_ref[:, part] = dot(jnp.concatenate(sides, 1), kept[b])
        return 0

    lax.fori_loop(0, leaf_dev, near_sum, 0, unroll=2)

    top = levels - 1
    send_u(top, partner(1 << top)[1]).wait_recv()
    down = dot(sib_u[top], across_blocks[top % 2]).astype(BF16)
    for k in range(levels - 2, -1, -1):
        down = (beside[k] + dot(down, own_blocks[k]) * totals[k, 0:1, :]).astype(BF16)

    def far(b, _):
        part = pl.ds(pl.multiple_of(b * leaf, leaf), leaf)
        out_ref[:, part] += dot(down, block0[:, part]) * total0[:, part]
        return 0

    lax.fori_loop(0, leaf_dev, far, 0, unroll=4)

    for k in range(levels):
        peer = partner(1 << k)[1]
        send_x(k, peer).wait_send()
        send_u(k, peer).wait_send()

    def sent(j, _):
        @pl.when(has_right)
        def _():
            piece(j, 0).wait_send()

        @pl.when(has_left)
        def _():
            piece(j, 1).wait_send()

        return 0

    lax.fori_loop(0, leaf_dev, sent, 0)

    @pl.when(has_right)
    def _():
        rightward.wait_send()

    @pl.when(has_left)
    def _():
        leftward.wait_send()


def body(points, charges, near_leaves, skel_device, skel_tree):
    inner_levels = lax.axis_size("inner").bit_length() - 1
    outer_levels = lax.axis_size("outer").bit_length() - 1
    levels = inner_levels + outer_levels
    n, size = points.shape[1], skel_device.shape[1]
    leaf_dev = near_leaves.shape[0]
    leaf = n // leaf_dev
    coordinates = pltpu.VMEM((levels, DIM, size), BF16)
    loads = pltpu.VMEM((levels, NRHS, size), BF16)
    blocks = pltpu.VMEM((levels, size, size), BF16)
    pair = pltpu.VMEM((2, size, size), BF16)
    each = pltpu.SemaphoreType.DMA((levels,))
    return pl.pallas_call(
        functools.partial(kernel, inner_levels, outer_levels),
        out_shape=jax.ShapeDtypeStruct((NRHS, n), F32),
        in_specs=[pl.BlockSpec(memory_space=pltpu.HBM)] * 5,
        out_specs=pl.BlockSpec(memory_space=pltpu.VMEM),
        scratch_shapes=[
            pltpu.SMEM(near_leaves.shape, jnp.int32),
            pltpu.VMEM(skel_device.shape, jnp.int32),
            pltpu.VMEM(skel_tree.shape, jnp.int32),
            pltpu.VMEM((DIM, 3 * n), BF16),
            pltpu.VMEM(charges.shape, BF16),
            pltpu.VMEM((3 * leaf_dev, NRHS, leaf), BF16),
            pltpu.VMEM((3 * leaf_dev, leaf, DEPTH), BF16),
            pltpu.VMEM((DEPTH, n), BF16),
            pltpu.VMEM((size, n), BF16),
            pltpu.VMEM((1, n), F32),
            pltpu.VMEM((NRHS, size), F32),
            coordinates, coordinates, loads, loads, blocks, pair, pair,
            pltpu.VMEM((levels, 2, size), F32),
            pltpu.VMEM((levels, NRHS, size), F32),
            pltpu.VMEM((leaf_dev, near_leaves.shape[1] * leaf, leaf), BF16),
            pltpu.SemaphoreType.DMA((2,)),
            pltpu.SemaphoreType.DMA((2,)),
            pltpu.SemaphoreType.DMA((2, leaf_dev)),
            pltpu.SemaphoreType.DMA((2, leaf_dev)),
            each, each, each, each,
            pltpu.SemaphoreType.DMA((5,)),
        ],
        compiler_params=pltpu.CompilerParams(
            collective_id=0, has_side_effects=True, vmem_limit_bytes=60 << 20
        ),
        name="skeleton_matvec",
    )(near_leaves, points, charges, skel_device, skel_tree)


def solution(mesh):
    return jax.shard_map(
        body,
        mesh=mesh,
        in_specs=(
            P(None, ("outer", "inner")),
            P(None, ("outer", "inner")),
            P(("outer", "inner"), None),
            P(("outer", "inner"), None),
            P(("outer", "inner"), None, None),
        ),
        out_specs=P(None, ("outer", "inner")),
        check_vma=False,
    )
```

```python
import functools

import jax
import jax.numpy as jnp
from jax import lax
from jax.experimental import pallas as pl
from jax.experimental.pallas import tpu as pltpu
from jax.sharding import PartitionSpec as P

DIM = 16
NRHS = 64
DEPTH = 64
GAMMA = 0.125
LOG2E = 1.4426950408889634
MESH = pl.DeviceIdType.MESH
F32 = jnp.float32
BF16 = jnp.bfloat16


def split3(value):
    high = value.astype(BF16).astype(F32)
    rest = value - high
    middle = rest.astype(BF16).astype(F32)
    return [high, middle, rest - middle]


def norms(x32):
    return split3(-(GAMMA * LOG2E) * jnp.sum(x32 * x32, 0, keepdims=True))


def padding(x32):
    return [jnp.zeros((DEPTH - 3 * DIM - 6, x32.shape[1]), F32)]


def row_side(x):
    x32 = x.astype(F32)
    ones = jnp.ones((1, x32.shape[1]), F32)
    parts = split3((2.0 * GAMMA * LOG2E) * x32) + norms(x32) + [ones] * 3 + padding(x32)
    return jnp.concatenate(parts, 0).T.astype(BF16)


def column_side(x):
    x32 = x.astype(F32)
    ones = jnp.ones((1, x32.shape[1]), F32)
    parts = [x32] * 3 + [ones] * 3 + norms(x32) + padding(x32)
    return jnp.concatenate(parts, 0).astype(BF16)


def dot(left, right):
    return jnp.dot(left, right, preferred_element_type=F32)


def dot_nt(left, right):
    return lax.dot_general(left, right, (((1,), (1,)), ((), ())), preferred_element_type=F32)


def gaussian(rows, columns):
    return jnp.exp2(dot(rows, columns)).astype(BF16)


def column_sums(block):
    return jnp.sum(block.astype(F32), 0, keepdims=True)


LANES = 128


def picked(source, chosen):
    depth, blocks = source.shape[0], source.shape[1] // LANES
    stacked = jnp.concatenate([source[:, i * LANES : (i + 1) * LANES] for i in range(blocks)], 0)
    lane, block = chosen & (LANES - 1), chosen >> (LANES.bit_length() - 1)
    index = lax.broadcasted_iota(jnp.int32, (LANES, chosen.shape[1]), 0)
    inside = dot(stacked, jnp.where(index == lane, 1.0, 0.0).astype(BF16))
    total = jnp.zeros((depth, chosen.shape[1]), F32)
    for i in range(blocks):
        total = total + jnp.where(block == i, inside[i * depth : (i + 1) * depth], 0.0)
    return total.astype(BF16)


def kernel(
    inner_levels, outer_levels, near_hbm, x_hbm, q_hbm, device_hbm, tree_hbm, out_hbm,
    near_ref, device_ref, tree_ref, x_all, q_ref, leaves_q, rows, cols, block0, total0, acc,
    own_x, sib_x, own_u, sib_u, own_blocks, sib_block, across_blocks, totals, beside, kept, out_ref,
    halo_send, halo_recv, piece_send, piece_recv, x_send, x_recv, u_send, u_recv, local_sem, out_sem,
):
    inner = 1 << inner_levels
    levels = inner_levels + outer_levels
    outer_id, inner_id = lax.axis_index("outer"), lax.axis_index("inner")
    count = inner << outer_levels
    position = outer_id * inner + inner_id
    n = x_hbm.shape[1]
    leaf_dev, n_near = near_ref.shape
    leaf = n // leaf_dev
    size = device_ref.shape[1]
    has_left, has_right = position > 0, position < count - 1
    left, right = jnp.maximum(position - 1, 0), jnp.minimum(position + 1, count - 1)
    left_id = (left // inner, left % inner)
    right_id = (right // inner, right % inner)

    def partner(step):
        bit = (position // step) % 2
        other = position + (1 - 2 * bit) * step
        return bit, (other // inner, other % inner)

    mine = pl.ds(n, n)
    sources = (x_hbm, device_hbm, q_hbm, tree_hbm, near_hbm)
    targets = (x_all.at[:, mine], device_ref, q_ref, tree_ref, near_ref)
    loads = [
        pltpu.make_async_copy(source, target, local_sem.at[i])
        for i, (source, target) in enumerate(zip(sources, targets))
    ]
    for load in loads:
        load.start()

    barrier = pltpu.get_barrier_semaphore()
    for k in range(levels):
        pl.semaphore_signal(barrier, inc=1, device_id=partner(1 << k)[1], device_id_type=MESH)

    @pl.when(has_left)
    def _():
        pl.semaphore_signal(barrier, inc=1, device_id=left_id, device_id_type=MESH)

    @pl.when(has_right)
    def _():
        pl.semaphore_signal(barrier, inc=1, device_id=right_id, device_id_type=MESH)

    def halo(source, target, send, recv, peer):
        return pltpu.make_async_remote_copy(
            src_ref=source, dst_ref=target, send_sem=send, recv_sem=recv,
            device_id=peer, device_id_type=MESH,
        )

    first, last = pl.ds(0, n), pl.ds(2 * n, n)
    rightward = halo(x_hbm, x_all.at[:, first], halo_send.at[0], halo_recv.at[0], right_id)
    leftward = halo(x_hbm, x_all.at[:, last], halo_send.at[1], halo_recv.at[1], left_id)

    def piece(j, side):
        part = pl.ds(pl.multiple_of(j * leaf, leaf), leaf)
        return halo(
            q_hbm.at[:, part], leaves_q.at[2 * side * leaf_dev + j], piece_send.at[side, j],
            piece_recv.at[side, j], (right_id, left_id)[side],
        )

    def feed(j):
        @pl.when(has_right)
        def _():
            piece(j, 0).start()

        @pl.when(has_left)
        def _():
            piece(j, 1).start()

    def exchange(source, target, send, recv, k, peer):
        return pltpu.make_async_remote_copy(
            src_ref=source.at[k], dst_ref=target.at[k], send_sem=send.at[k],
            recv_sem=recv.at[k], device_id=peer, device_id_type=MESH,
        )

    def send_x(k, peer):
        return exchange(own_x, sib_x, x_send, x_recv, k, peer)

    def send_u(k, peer):
        return exchange(own_u, sib_u, u_send, u_recv, k, peer)

    loads[0].wait()
    loads[1].wait()
    base_x = picked(x_all[:, mine], device_ref[...])
    own_x[0] = base_x

    def columns_of(j, _):
        source = pl.ds(pl.multiple_of(n + j * leaf, leaf), leaf)
        part = pl.ds(pl.multiple_of(j * leaf, leaf), leaf)
        cols[:, part] = column_side(x_all[:, source])
        return 0

    lax.fori_loop(0, leaf_dev, columns_of, 0, unroll=4)

    def prepare(start):
        def one(j, _):
            part = pl.ds(pl.multiple_of((start + j) * leaf, leaf), leaf)
            rows[start + j] = row_side(x_all[:, part])
            return 0

        lax.fori_loop(0, leaf_dev, one, 0, unroll=8)

    def own_leaves(j, _):
        part = pl.ds(pl.multiple_of(j * leaf, leaf), leaf)
        leaves_q[leaf_dev + j] = q_ref[:, part]
        return 0

    loads[2].wait()
    lax.fori_loop(0, leaf_dev, own_leaves, 0, unroll=4)
    prepare(leaf_dev)

    beside_us = (position + count - 1) // count + 1 - (position + 1) // count
    pl.semaphore_wait(barrier, levels + beside_us)
    send_x(0, partner(1)[1]).start()

    @pl.when(has_right)
    def _():
        rightward.start()

    @pl.when(has_left)
    def _():
        leftward.start()

    chunk = 512
    wide = n // chunk
    base_rows = row_side(base_x)
    acc[...] = jnp.zeros_like(acc)

    def chunk_of(c):
        return pl.ds(pl.multiple_of(c * chunk, chunk), chunk)

    def base_block(c):
        part = chunk_of(c)
        block = gaussian(base_rows, cols[:, part])
        block0[:, part] = block
        total0[:, part] = 1.0 / column_sums(block)

    def base_sum(c):
        part = chunk_of(c)
        weights = (q_ref[:, part].astype(F32) * total0[:, part]).astype(BF16)
        acc[...] += dot_nt(weights, block0[:, part])

    def base(c, _):
        base_sum(c - 1)
        base_block(c)
        return 0

    for load in loads[3:]:
        load.wait()
    base_block(0)
    lax.fori_loop(1, wide, base, 0)
    base_sum(wide - 1)
    own_u[0] = acc[...].astype(BF16)
    send_u(0, partner(1)[1]).start()
    fed = 0

    def tree_blocks(k, bit, peer_above):
        own, sib = own_x[k], sib_x[k]
        own_cols = column_side(own)
        shifted = tree_ref[0, pl.ds(k, 1), :] + bit * size
        chosen = jnp.where(shifted >= 2 * size, shifted - 2 * size, shifted)
        parent = picked(jnp.concatenate([own, sib], 1), chosen)
        own_x[k + 1] = parent
        send_x(k + 1, peer_above).start()
        parent_rows = row_side(parent)
        block = gaussian(parent_rows, own_cols)
        own_blocks[k] = block
        totals[k, 0:1, :] = 1.0 / column_sums(block)
        block = gaussian(parent_rows, column_side(sib))
        sib_block[k % 2] = block
        totals[k, 1:2, :] = 1.0 / column_sums(block)

    def across(k):
        across_blocks[k % 2] = gaussian(row_side(sib_x[k]), column_side(own_x[k]))

    def raised(values, k, which, block):
        return dot_nt((values.astype(F32) * totals[k, which : which + 1, :]).astype(BF16), block)

    def number_of(b, turn):
        number = near_ref[b, turn] - (position - 1) * leaf_dev
        return jnp.minimum(jnp.maximum(number, 0), 3 * leaf_dev - 1)

    def near_weights(b, _):
        @pl.when(ahead + b < leaf_dev)
        def _():
            feed(ahead + b)

        columns = cols[:, pl.ds(pl.multiple_of(b * leaf, leaf), leaf)]
        for turn in range(n_near):
            kept[b, turn * leaf : (turn + 1) * leaf, :] = gaussian(rows[number_of(b, turn)], columns)
        return 0

    send_x(0, partner(1)[1]).wait_recv()
    feed(fed)
    tree_blocks(0, partner(1)[0], partner(2)[1])
    across(0)
    feed(fed + 1)

    @pl.when(has_left)
    def _():
        rightward.wait_recv()

    feed(fed + 2)
    prepare(0)

    @pl.when(has_right)
    def _():
        leftward.wait_recv()

    feed(fed + 3)
    prepare(2 * leaf_dev)
    ahead = fed + 4
    share = max(1, 4 * 4 // (levels - 1))

    def level(k, step):
        _, peer = partner(step)
        bit, peer_above = partner(2 * step)
        lax.fori_loop(k * share, (k + 1) * share, near_weights, 0)
        send_x(k + 1, peer_above).wait_recv()

        @pl.when(k < levels - 2)
        def _():
            tree_blocks(k + 1, bit, partner(jnp.minimum(4 * step, count // 2))[1])

        across(k + 1)
        part = raised(own_u[k], k, 0, own_blocks[k])
        send_u(k, peer).wait_recv()
        own_u[k + 1] = (part + raised(sib_u[k], k, 1, sib_block[k % 2])).astype(BF16)
        send_u(k + 1, peer_above).start()
        beside[k] = dot(sib_u[k], across_blocks[k % 2])
        return 2 * step

    lax.fori_loop(0, levels - 1, level, jnp.int32(1))
    done = (levels - 1) * share
    if done < leaf_dev:
        lax.fori_loop(done, leaf_dev, near_weights, 0)

    def arrived(j, _):
        @pl.when(has_left)
        def _():
            piece(j, 0).wait_recv()

        @pl.when(has_right)
        def _():
            piece(j, 1).wait_recv()

        return 0

    lax.fori_loop(0, leaf_dev, arrived, 0)

    def near_sum(b, _):
        part = pl.ds(pl.multiple_of(b * leaf, leaf), leaf)
        sides = [leaves_q[number_of(b, turn)] for turn in range(n_near)]
        out_ref[:, part] = dot(jnp.concatenate(sides, 1), kept[b])
        return 0

    lax.fori_loop(0, leaf_dev, near_sum, 0, unroll=4)

    top = levels - 1
    send_u(top, partner(1 << top)[1]).wait_recv()
    down = dot(sib_u[top], across_blocks[top % 2]).astype(BF16)
    for k in range(levels - 2, -1, -1):
        down = (beside[k] + dot(down, own_blocks[k]) * totals[k, 0:1, :]).astype(BF16)

    def store(c):
        return pltpu.make_async_copy(out_ref.at[:, chunk_of(c)], out_hbm.at[:, chunk_of(c)], out_sem.at[c])

    def far(c, _):
        part = chunk_of(c)
        out_ref[:, part] += dot(down, block0[:, part]) * total0[:, part]
        store(c).start()
        return 0

    lax.fori_loop(0, wide, far, 0, unroll=8)

    for k in range(levels):
        peer = partner(1 << k)[1]
        send_x(k, peer).wait_send()
        send_u(k, peer).wait_send()

    for c in range(wide):
        store(c).wait()

    def sent(j, _):
        @pl.when(has_right)
        def _():
            piece(j, 0).wait_send()

        @pl.when(has_left)
        def _():
            piece(j, 1).wait_send()

        return 0

    lax.fori_loop(0, leaf_dev, sent, 0)

    @pl.when(has_right)
    def _():
        rightward.wait_send()

    @pl.when(has_left)
    def _():
        leftward.wait_send()


def body(points, charges, near_leaves, skel_device, skel_tree):
    inner_levels = lax.axis_size("inner").bit_length() - 1
    outer_levels = lax.axis_size("outer").bit_length() - 1
    levels = inner_levels + outer_levels
    n, size = points.shape[1], skel_device.shape[1]
    leaf_dev = near_leaves.shape[0]
    leaf = n // leaf_dev
    coordinates = pltpu.VMEM((levels, DIM, size), BF16)
    loads = pltpu.VMEM((levels, NRHS, size), BF16)
    blocks = pltpu.VMEM((levels, size, size), BF16)
    pair = pltpu.VMEM((2, size, size), BF16)
    each = pltpu.SemaphoreType.DMA((levels,))
    return pl.pallas_call(
        functools.partial(kernel, inner_levels, outer_levels),
        out_shape=jax.ShapeDtypeStruct((NRHS, n), F32),
        in_specs=[pl.BlockSpec(memory_space=pltpu.HBM)] * 5,
        out_specs=pl.BlockSpec(memory_space=pltpu.HBM),
        scratch_shapes=[
            pltpu.SMEM(near_leaves.shape, jnp.int32),
            pltpu.VMEM(skel_device.shape, jnp.int32),
            pltpu.VMEM(skel_tree.shape, jnp.int32),
            pltpu.VMEM((DIM, 3 * n), BF16),
            pltpu.VMEM(charges.shape, BF16),
            pltpu.VMEM((3 * leaf_dev, NRHS, leaf), BF16),
            pltpu.VMEM((3 * leaf_dev, leaf, DEPTH), BF16),
            pltpu.VMEM((DEPTH, n), BF16),
            pltpu.VMEM((size, n), BF16),
            pltpu.VMEM((1, n), F32),
            pltpu.VMEM((NRHS, size), F32),
            coordinates, coordinates, loads, loads, blocks, pair, pair,
            pltpu.VMEM((levels, 2, size), F32),
            pltpu.VMEM((levels, NRHS, size), F32),
            pltpu.VMEM((leaf_dev, near_leaves.shape[1] * leaf, leaf), BF16),
            pltpu.VMEM((NRHS, n), F32),
            pltpu.SemaphoreType.DMA((2,)),
            pltpu.SemaphoreType.DMA((2,)),
            pltpu.SemaphoreType.DMA((2, leaf_dev)),
            pltpu.SemaphoreType.DMA((2, leaf_dev)),
            each, each, each, each,
            pltpu.SemaphoreType.DMA((5,)),
            pltpu.SemaphoreType.DMA((n // 512,)),
        ],
        compiler_params=pltpu.CompilerParams(
            collective_id=0, has_side_effects=True, vmem_limit_bytes=60 << 20
        ),
        name="skeleton_matvec",
    )(near_leaves, points, charges, skel_device, skel_tree)


def solution(mesh):
    return jax.shard_map(
        body,
        mesh=mesh,
        in_specs=(
            P(None, ("outer", "inner")),
            P(None, ("outer", "inner")),
            P(("outer", "inner"), None),
            P(("outer", "inner"), None),
            P(("outer", "inner"), None, None),
        ),
        out_specs=P(None, ("outer", "inner")),
        check_vma=False,
    )
```

```python
import functools

import jax
import jax.numpy as jnp
from jax import lax
from jax.experimental import pallas as pl
from jax.experimental.pallas import tpu as pltpu
from jax.sharding import PartitionSpec as P

DIM = 16
NRHS = 64
DEPTH = 64
GAMMA = 0.125
LOG2E = 1.4426950408889634
MESH = pl.DeviceIdType.MESH
F32 = jnp.float32
BF16 = jnp.bfloat16


def split3(value):
    high = value.astype(BF16).astype(F32)
    rest = value - high
    middle = rest.astype(BF16).astype(F32)
    return [high, middle, rest - middle]


def norms(x32):
    return split3(-(GAMMA * LOG2E) * jnp.sum(x32 * x32, 0, keepdims=True))


def padding(x32):
    return [jnp.zeros((DEPTH - 3 * DIM - 6, x32.shape[1]), F32)]


def row_side(x):
    x32 = x.astype(F32)
    ones = jnp.ones((1, x32.shape[1]), F32)
    parts = split3((2.0 * GAMMA * LOG2E) * x32) + norms(x32) + [ones] * 3 + padding(x32)
    return jnp.concatenate(parts, 0).T.astype(BF16)


def column_side(x):
    x32 = x.astype(F32)
    ones = jnp.ones((1, x32.shape[1]), F32)
    parts = [x32] * 3 + [ones] * 3 + norms(x32) + padding(x32)
    return jnp.concatenate(parts, 0).astype(BF16)


def dot(left, right):
    return jnp.dot(left, right, preferred_element_type=F32)


def dot_nt(left, right):
    return lax.dot_general(left, right, (((1,), (1,)), ((), ())), preferred_element_type=F32)


def gaussian(rows, columns):
    return jnp.exp2(dot(rows, columns)).astype(BF16)


def column_sums(block):
    return jnp.sum(block.astype(F32), 0, keepdims=True)


LANES = 128


def picked(source, chosen):
    depth, blocks = source.shape[0], source.shape[1] // LANES
    stacked = jnp.concatenate([source[:, i * LANES : (i + 1) * LANES] for i in range(blocks)], 0)
    lane, block = chosen & (LANES - 1), chosen >> (LANES.bit_length() - 1)
    index = lax.broadcasted_iota(jnp.int32, (LANES, chosen.shape[1]), 0)
    inside = dot(stacked, jnp.where(index == lane, 1.0, 0.0).astype(BF16))
    total = jnp.zeros((depth, chosen.shape[1]), F32)
    for i in range(blocks):
        total = total + jnp.where(block == i, inside[i * depth : (i + 1) * depth], 0.0)
    return total.astype(BF16)


def kernel(
    inner_levels, outer_levels, near_hbm, x_hbm, q_hbm, device_hbm, tree_hbm, out_hbm,
    near_ref, device_ref, tree_ref, x_all, q_ref, leaves_q, rows, cols, block0, total0, acc,
    own_x, sib_x, own_u, sib_u, own_blocks, sib_block, across_blocks, totals, beside, kept, out_ref,
    halo_send, halo_recv, piece_send, piece_recv, x_send, x_recv, u_send, u_recv, local_sem, out_sem,
):
    inner = 1 << inner_levels
    levels = inner_levels + outer_levels
    outer_id, inner_id = lax.axis_index("outer"), lax.axis_index("inner")
    count = inner << outer_levels
    position = outer_id * inner + inner_id
    n = x_hbm.shape[1]
    leaf_dev, n_near = near_ref.shape
    leaf = n // leaf_dev
    size = device_ref.shape[1]
    has_left, has_right = position > 0, position < count - 1
    left, right = jnp.maximum(position - 1, 0), jnp.minimum(position + 1, count - 1)
    left_id = (left // inner, left % inner)
    right_id = (right // inner, right % inner)

    def partner(step):
        bit = (position // step) % 2
        other = position + (1 - 2 * bit) * step
        return bit, (other // inner, other % inner)

    mine = pl.ds(n, n)
    sources = (x_hbm, device_hbm, q_hbm, tree_hbm, near_hbm)
    targets = (x_all.at[:, mine], device_ref, q_ref, tree_ref, near_ref)
    loads = [
        pltpu.make_async_copy(source, target, local_sem.at[i])
        for i, (source, target) in enumerate(zip(sources, targets))
    ]
    for load in loads:
        load.start()

    barrier = pltpu.get_barrier_semaphore()
    for k in range(levels):
        pl.semaphore_signal(barrier, inc=1, device_id=partner(1 << k)[1], device_id_type=MESH)

    @pl.when(has_left)
    def _():
        pl.semaphore_signal(barrier, inc=1, device_id=left_id, device_id_type=MESH)

    @pl.when(has_right)
    def _():
        pl.semaphore_signal(barrier, inc=1, device_id=right_id, device_id_type=MESH)

    def halo(source, target, send, recv, peer):
        return pltpu.make_async_remote_copy(
            src_ref=source, dst_ref=target, send_sem=send, recv_sem=recv,
            device_id=peer, device_id_type=MESH,
        )

    first, last = pl.ds(0, n), pl.ds(2 * n, n)
    rightward = halo(x_hbm, x_all.at[:, first], halo_send.at[0], halo_recv.at[0], right_id)
    leftward = halo(x_hbm, x_all.at[:, last], halo_send.at[1], halo_recv.at[1], left_id)

    def piece(j, side):
        part = pl.ds(pl.multiple_of(j * leaf, leaf), leaf)
        return halo(
            q_hbm.at[:, part], leaves_q.at[2 * side * leaf_dev + j], piece_send.at[side, j],
            piece_recv.at[side, j], (right_id, left_id)[side],
        )

    def feed(j):
        @pl.when(has_right)
        def _():
            piece(j, 0).start()

        @pl.when(has_left)
        def _():
            piece(j, 1).start()

    def exchange(source, target, send, recv, k, peer):
        return pltpu.make_async_remote_copy(
            src_ref=source.at[k], dst_ref=target.at[k], send_sem=send.at[k],
            recv_sem=recv.at[k], device_id=peer, device_id_type=MESH,
        )

    def send_x(k, peer):
        return exchange(own_x, sib_x, x_send, x_recv, k, peer)

    def send_u(k, peer):
        return exchange(own_u, sib_u, u_send, u_recv, k, peer)

    loads[0].wait()
    loads[1].wait()
    base_x = picked(x_all[:, mine], device_ref[...])
    own_x[0] = base_x

    def prepare(start):
        def one(j, _):
            part = pl.ds(pl.multiple_of((start + j) * leaf, leaf), leaf)
            rows[start + j] = row_side(x_all[:, part])
            return 0

        lax.fori_loop(0, leaf_dev, one, 0, unroll=8)

    def own_leaves(j, _):
        part = pl.ds(pl.multiple_of(j * leaf, leaf), leaf)
        leaves_q[leaf_dev + j] = q_ref[:, part]
        return 0

    loads[2].wait()
    lax.fori_loop(0, leaf_dev, own_leaves, 0, unroll=4)
    prepare(leaf_dev)

    beside_us = (position + count - 1) // count + 1 - (position + 1) // count
    pl.semaphore_wait(barrier, levels + beside_us)
    send_x(0, partner(1)[1]).start()

    @pl.when(has_right)
    def _():
        rightward.start()

    @pl.when(has_left)
    def _():
        leftward.start()

    def columns_of(j, _):
        source = pl.ds(pl.multiple_of(n + j * leaf, leaf), leaf)
        part = pl.ds(pl.multiple_of(j * leaf, leaf), leaf)
        cols[:, part] = column_side(x_all[:, source])
        return 0

    lax.fori_loop(0, leaf_dev, columns_of, 0, unroll=4)

    chunk = 512
    wide = n // chunk
    base_rows = row_side(base_x)
    acc[...] = jnp.zeros_like(acc)

    def chunk_of(c):
        return pl.ds(pl.multiple_of(c * chunk, chunk), chunk)

    def base_block(c):
        part = chunk_of(c)
        block = gaussian(base_rows, cols[:, part])
        block0[:, part] = block
        total0[:, part] = 1.0 / column_sums(block)

    def base_sum(c):
        part = chunk_of(c)
        weights = (q_ref[:, part].astype(F32) * total0[:, part]).astype(BF16)
        acc[...] += dot_nt(weights, block0[:, part])

    def base(c, _):
        base_sum(c - 1)
        base_block(c)
        return 0

    for load in loads[3:]:
        load.wait()
    base_block(0)
    lax.fori_loop(1, wide, base, 0, unroll=True)
    base_sum(wide - 1)
    own_u[0] = acc[...].astype(BF16)
    send_u(0, partner(1)[1]).start()
    fed = 0

    def tree_blocks(k, bit, peer_above):
        own, sib = own_x[k], sib_x[k]
        own_cols = column_side(own)
        shifted = tree_ref[0, pl.ds(k, 1), :] + bit * size
        chosen = jnp.where(shifted >= 2 * size, shifted - 2 * size, shifted)
        parent = picked(jnp.concatenate([own, sib], 1), chosen)
        own_x[k + 1] = parent
        send_x(k + 1, peer_above).start()
        parent_rows = row_side(parent)
        block = gaussian(parent_rows, own_cols)
        own_blocks[k] = block
        totals[k, 0:1, :] = 1.0 / column_sums(block)
        block = gaussian(parent_rows, column_side(sib))
        sib_block[k % 2] = block
        totals[k, 1:2, :] = 1.0 / column_sums(block)

    def across(k):
        across_blocks[k % 2] = gaussian(row_side(sib_x[k]), column_side(own_x[k]))

    def raised(values, k, which, block):
        return dot_nt((values.astype(F32) * totals[k, which : which + 1, :]).astype(BF16), block)

    def number_of(b, turn):
        number = near_ref[b, turn] - (position - 1) * leaf_dev
        return jnp.minimum(jnp.maximum(number, 0), 3 * leaf_dev - 1)

    def near_weights(b, _):
        @pl.when(ahead + b < leaf_dev)
        def _():
            feed(ahead + b)

        columns = cols[:, pl.ds(pl.multiple_of(b * leaf, leaf), leaf)]
        for turn in range(n_near):
            kept[b, turn * leaf : (turn + 1) * leaf, :] = gaussian(rows[number_of(b, turn)], columns)
        return 0

    send_x(0, partner(1)[1]).wait_recv()
    feed(fed)
    tree_blocks(0, partner(1)[0], partner(2)[1])
    across(0)
    feed(fed + 1)

    @pl.when(has_left)
    def _():
        rightward.wait_recv()

    feed(fed + 2)
    prepare(0)

    @pl.when(has_right)
    def _():
        leftward.wait_recv()

    feed(fed + 3)
    prepare(2 * leaf_dev)
    ahead = fed + 4
    share = max(1, 4 * 4 // (levels - 1))

    def level(k, step):
        _, peer = partner(step)
        bit, peer_above = partner(2 * step)
        def several(i, _):
            for j in range(4):
                near_weights(k * share + 4 * i + j, 0)
            return 0

        lax.fori_loop(0, share // 4, several, 0)
        if share % 4:
            lax.fori_loop(k * share + share // 4 * 4, (k + 1) * share, near_weights, 0)
        send_x(k + 1, peer_above).wait_recv()

        @pl.when(k < levels - 2)
        def _():
            tree_blocks(k + 1, bit, partner(jnp.minimum(4 * step, count // 2))[1])

        across(k + 1)
        part = raised(own_u[k], k, 0, own_blocks[k])
        send_u(k, peer).wait_recv()
        own_u[k + 1] = (part + raised(sib_u[k], k, 1, sib_block[k % 2])).astype(BF16)
        send_u(k + 1, peer_above).start()
        beside[k] = dot(sib_u[k], across_blocks[k % 2])
        return 2 * step

    lax.fori_loop(0, levels - 1, level, jnp.int32(1))
    done = (levels - 1) * share
    if done < leaf_dev:
        lax.fori_loop(done, leaf_dev, near_weights, 0)

    def arrived(j, _):
        @pl.when(has_left)
        def _():
            piece(j, 0).wait_recv()

        @pl.when(has_right)
        def _():
            piece(j, 1).wait_recv()

        return 0

    lax.fori_loop(0, leaf_dev, arrived, 0)

    def near_sum(b, _):
        part = pl.ds(pl.multiple_of(b * leaf, leaf), leaf)
        sides = [leaves_q[number_of(b, turn)] for turn in range(n_near)]
        out_ref[:, part] = dot(jnp.concatenate(sides, 1), kept[b])
        return 0

    lax.fori_loop(0, leaf_dev, near_sum, 0, unroll=8)

    top = levels - 1
    send_u(top, partner(1 << top)[1]).wait_recv()
    down = dot(sib_u[top], across_blocks[top % 2]).astype(BF16)
    for k in range(levels - 2, -1, -1):
        down = (beside[k] + dot(down, own_blocks[k]) * totals[k, 0:1, :]).astype(BF16)

    def store(c):
        return pltpu.make_async_copy(out_ref.at[:, chunk_of(c)], out_hbm.at[:, chunk_of(c)], out_sem.at[c])

    def far(c, _):
        part = chunk_of(c)
        out_ref[:, part] += dot(down, block0[:, part]) * total0[:, part]
        store(c).start()
        return 0

    lax.fori_loop(0, wide, far, 0, unroll=8)

    for k in range(levels):
        peer = partner(1 << k)[1]
        send_x(k, peer).wait_send()
        send_u(k, peer).wait_send()

    for c in range(wide):
        store(c).wait()

    def sent(j, _):
        @pl.when(has_right)
        def _():
            piece(j, 0).wait_send()

        @pl.when(has_left)
        def _():
            piece(j, 1).wait_send()

        return 0

    lax.fori_loop(0, leaf_dev, sent, 0)

    @pl.when(has_right)
    def _():
        rightward.wait_send()

    @pl.when(has_left)
    def _():
        leftward.wait_send()


def body(points, charges, near_leaves, skel_device, skel_tree):
    inner_levels = lax.axis_size("inner").bit_length() - 1
    outer_levels = lax.axis_size("outer").bit_length() - 1
    levels = inner_levels + outer_levels
    n, size = points.shape[1], skel_device.shape[1]
    leaf_dev = near_leaves.shape[0]
    leaf = n // leaf_dev
    coordinates = pltpu.VMEM((levels, DIM, size), BF16)
    loads = pltpu.VMEM((levels, NRHS, size), BF16)
    blocks = pltpu.VMEM((levels, size, size), BF16)
    pair = pltpu.VMEM((2, size, size), BF16)
    each = pltpu.SemaphoreType.DMA((levels,))
    return pl.pallas_call(
        functools.partial(kernel, inner_levels, outer_levels),
        out_shape=jax.ShapeDtypeStruct((NRHS, n), F32),
        in_specs=[pl.BlockSpec(memory_space=pltpu.HBM)] * 5,
        out_specs=pl.BlockSpec(memory_space=pltpu.HBM),
        scratch_shapes=[
            pltpu.SMEM(near_leaves.shape, jnp.int32),
            pltpu.VMEM(skel_device.shape, jnp.int32),
            pltpu.VMEM(skel_tree.shape, jnp.int32),
            pltpu.VMEM((DIM, 3 * n), BF16),
            pltpu.VMEM(charges.shape, BF16),
            pltpu.VMEM((3 * leaf_dev, NRHS, leaf), BF16),
            pltpu.VMEM((3 * leaf_dev, leaf, DEPTH), BF16),
            pltpu.VMEM((DEPTH, n), BF16),
            pltpu.VMEM((size, n), BF16),
            pltpu.VMEM((1, n), F32),
            pltpu.VMEM((NRHS, size), F32),
            coordinates, coordinates, loads, loads, blocks, pair, pair,
            pltpu.VMEM((levels, 2, size), F32),
            pltpu.VMEM((levels, NRHS, size), F32),
            pltpu.VMEM((leaf_dev, near_leaves.shape[1] * leaf, leaf), BF16),
            pltpu.VMEM((NRHS, n), F32),
            pltpu.SemaphoreType.DMA((2,)),
            pltpu.SemaphoreType.DMA((2,)),
            pltpu.SemaphoreType.DMA((2, leaf_dev)),
            pltpu.SemaphoreType.DMA((2, leaf_dev)),
            each, each, each, each,
            pltpu.SemaphoreType.DMA((5,)),
            pltpu.SemaphoreType.DMA((n // 512,)),
        ],
        compiler_params=pltpu.CompilerParams(
            collective_id=0, has_side_effects=True, vmem_limit_bytes=60 << 20
        ),
        name="skeleton_matvec",
    )(near_leaves, points, charges, skel_device, skel_tree)


def solution(mesh):
    return jax.shard_map(
        body,
        mesh=mesh,
        in_specs=(
            P(None, ("outer", "inner")),
            P(None, ("outer", "inner")),
            P(("outer", "inner"), None),
            P(("outer", "inner"), None),
            P(("outer", "inner"), None, None),
        ),
        out_specs=P(None, ("outer", "inner")),
        check_vma=False,
    )
```

```python
import functools

import jax
import jax.numpy as jnp
from jax import lax
from jax.experimental import pallas as pl
from jax.experimental.pallas import tpu as pltpu
from jax.sharding import PartitionSpec as P

DIM = 16
NRHS = 64
DEPTH = 64
GAMMA = 0.125
LOG2E = 1.4426950408889634
MESH = pl.DeviceIdType.MESH
F32 = jnp.float32
BF16 = jnp.bfloat16


def split3(value):
    high = value.astype(BF16).astype(F32)
    rest = value - high
    middle = rest.astype(BF16).astype(F32)
    return [high, middle, rest - middle]


def norms(x32):
    return split3(-(GAMMA * LOG2E) * jnp.sum(x32 * x32, 0, keepdims=True))


def padding(x32):
    return [jnp.zeros((DEPTH - 3 * DIM - 6, x32.shape[1]), F32)]


def row_side(x):
    x32 = x.astype(F32)
    ones = jnp.ones((1, x32.shape[1]), F32)
    parts = split3((2.0 * GAMMA * LOG2E) * x32) + norms(x32) + [ones] * 3 + padding(x32)
    return jnp.concatenate(parts, 0).T.astype(BF16)


def column_side(x):
    x32 = x.astype(F32)
    ones = jnp.ones((1, x32.shape[1]), F32)
    parts = [x32] * 3 + [ones] * 3 + norms(x32) + padding(x32)
    return jnp.concatenate(parts, 0).astype(BF16)


def dot(left, right):
    return jnp.dot(left, right, preferred_element_type=F32)


def dot_nt(left, right):
    return lax.dot_general(left, right, (((1,), (1,)), ((), ())), preferred_element_type=F32)


def gaussian(rows, columns):
    return jnp.exp2(dot(rows, columns)).astype(BF16)


def column_sums(block):
    return jnp.sum(block.astype(F32), 0, keepdims=True)


LANES = 128


def picked(source, chosen):
    depth, blocks = source.shape[0], source.shape[1] // LANES
    stacked = jnp.concatenate([source[:, i * LANES : (i + 1) * LANES] for i in range(blocks)], 0)
    lane, block = chosen & (LANES - 1), chosen >> (LANES.bit_length() - 1)
    index = lax.broadcasted_iota(jnp.int32, (LANES, chosen.shape[1]), 0)
    inside = dot(stacked, jnp.where(index == lane, 1.0, 0.0).astype(BF16))
    total = jnp.zeros((depth, chosen.shape[1]), F32)
    for i in range(blocks):
        total = total + jnp.where(block == i, inside[i * depth : (i + 1) * depth], 0.0)
    return total.astype(BF16)


def kernel(
    inner_levels, outer_levels, near_hbm, x_hbm, q_hbm, device_hbm, tree_hbm, out_hbm,
    near_ref, device_ref, tree_ref, x_all, q_ref, leaves_q, rows, cols, block0, total0, acc,
    own_x, sib_x, own_u, sib_u, own_blocks, sib_block, across_blocks, totals, beside, kept, out_ref,
    halo_send, halo_recv, piece_send, piece_recv, x_send, x_recv, u_send, u_recv, local_sem, out_sem,
):
    inner = 1 << inner_levels
    levels = inner_levels + outer_levels
    outer_id, inner_id = lax.axis_index("outer"), lax.axis_index("inner")
    count = inner << outer_levels
    position = outer_id * inner + inner_id
    n = x_hbm.shape[1]
    leaf_dev, n_near = near_ref.shape
    leaf = n // leaf_dev
    size = device_ref.shape[1]
    has_left, has_right = position > 0, position < count - 1
    left, right = jnp.maximum(position - 1, 0), jnp.minimum(position + 1, count - 1)
    left_id = (left // inner, left % inner)
    right_id = (right // inner, right % inner)

    def partner(step):
        bit = (position // step) % 2
        other = position + (1 - 2 * bit) * step
        return bit, (other // inner, other % inner)

    mine = pl.ds(n, n)
    sources = (x_hbm, device_hbm, q_hbm, tree_hbm, near_hbm)
    targets = (x_all.at[:, mine], device_ref, q_ref, tree_ref, near_ref)
    loads = [
        pltpu.make_async_copy(source, target, local_sem.at[i])
        for i, (source, target) in enumerate(zip(sources, targets))
    ]
    for load in loads:
        load.start()

    barrier = pltpu.get_barrier_semaphore()
    for k in range(levels):
        pl.semaphore_signal(barrier, inc=1, device_id=partner(1 << k)[1], device_id_type=MESH)

    @pl.when(has_left)
    def _():
        pl.semaphore_signal(barrier, inc=1, device_id=left_id, device_id_type=MESH)

    @pl.when(has_right)
    def _():
        pl.semaphore_signal(barrier, inc=1, device_id=right_id, device_id_type=MESH)

    def halo(source, target, send, recv, peer):
        return pltpu.make_async_remote_copy(
            src_ref=source, dst_ref=target, send_sem=send, recv_sem=recv,
            device_id=peer, device_id_type=MESH,
        )

    first, last = pl.ds(0, n), pl.ds(2 * n, n)
    rightward = halo(x_hbm, x_all.at[:, first], halo_send.at[0], halo_recv.at[0], right_id)
    leftward = halo(x_hbm, x_all.at[:, last], halo_send.at[1], halo_recv.at[1], left_id)

    def piece(j, side):
        part = pl.ds(pl.multiple_of(j * leaf, leaf), leaf)
        return halo(
            q_hbm.at[:, part], leaves_q.at[2 * side * leaf_dev + j], piece_send.at[side, j],
            piece_recv.at[side, j], (right_id, left_id)[side],
        )

    def feed(j):
        @pl.when(has_right)
        def _():
            piece(j, 0).start()

        @pl.when(has_left)
        def _():
            piece(j, 1).start()

    def exchange(source, target, send, recv, k, peer):
        return pltpu.make_async_remote_copy(
            src_ref=source.at[k], dst_ref=target.at[k], send_sem=send.at[k],
            recv_sem=recv.at[k], device_id=peer, device_id_type=MESH,
        )

    def send_x(k, peer):
        return exchange(own_x, sib_x, x_send, x_recv, k, peer)

    def send_u(k, peer):
        return exchange(own_u, sib_u, u_send, u_recv, k, peer)

    loads[0].wait()
    loads[1].wait()
    base_x = picked(x_all[:, mine], device_ref[...])
    own_x[0] = base_x

    def prepare(start):
        def one(j, _):
            part = pl.ds(pl.multiple_of((start + j) * leaf, leaf), leaf)
            rows[start + j] = row_side(x_all[:, part])
            return 0

        lax.fori_loop(0, leaf_dev, one, 0, unroll=16)

    def own_leaves(j, _):
        part = pl.ds(pl.multiple_of(j * leaf, leaf), leaf)
        leaves_q[leaf_dev + j] = q_ref[:, part]
        return 0

    loads[2].wait()
    lax.fori_loop(0, leaf_dev, own_leaves, 0, unroll=4)
    prepare(leaf_dev)

    beside_us = (position + count - 1) // count + 1 - (position + 1) // count
    pl.semaphore_wait(barrier, levels + beside_us)
    send_x(0, partner(1)[1]).start()

    @pl.when(has_right)
    def _():
        rightward.start()

    @pl.when(has_left)
    def _():
        leftward.start()

    def columns_of(j, _):
        source = pl.ds(pl.multiple_of(n + j * leaf, leaf), leaf)
        part = pl.ds(pl.multiple_of(j * leaf, leaf), leaf)
        cols[:, part] = column_side(x_all[:, source])
        return 0

    lax.fori_loop(0, leaf_dev, columns_of, 0, unroll=4)

    chunk = 512
    wide = n // chunk
    base_rows = row_side(base_x)
    acc[...] = jnp.zeros_like(acc)

    def chunk_of(c):
        return pl.ds(pl.multiple_of(c * chunk, chunk), chunk)

    def base_block(c):
        part = chunk_of(c)
        block = gaussian(base_rows, cols[:, part])
        block0[:, part] = block
        total0[:, part] = 1.0 / column_sums(block)

    def base_sum(c):
        part = chunk_of(c)
        weights = (q_ref[:, part].astype(F32) * total0[:, part]).astype(BF16)
        acc[...] += dot_nt(weights, block0[:, part])

    def base(c, _):
        base_sum(c - 1)
        base_block(c)
        return 0

    for load in loads[3:]:
        load.wait()
    base_block(0)
    lax.fori_loop(1, wide, base, 0, unroll=True)
    base_sum(wide - 1)
    own_u[0] = acc[...].astype(BF16)
    send_u(0, partner(1)[1]).start()
    fed = 0

    def tree_blocks(k, bit, peer_above):
        own, sib = own_x[k], sib_x[k]
        own_cols = column_side(own)
        shifted = tree_ref[0, pl.ds(k, 1), :] + bit * size
        chosen = jnp.where(shifted >= 2 * size, shifted - 2 * size, shifted)
        parent = picked(jnp.concatenate([own, sib], 1), chosen)
        own_x[k + 1] = parent
        send_x(k + 1, peer_above).start()
        parent_rows = row_side(parent)
        block = gaussian(parent_rows, own_cols)
        own_blocks[k] = block
        totals[k, 0:1, :] = 1.0 / column_sums(block)
        block = gaussian(parent_rows, column_side(sib))
        sib_block[k % 2] = block
        totals[k, 1:2, :] = 1.0 / column_sums(block)

    def across(k):
        across_blocks[k % 2] = gaussian(row_side(sib_x[k]), column_side(own_x[k]))

    def raised(values, k, which, block):
        return dot_nt((values.astype(F32) * totals[k, which : which + 1, :]).astype(BF16), block)

    def number_of(b, turn):
        number = near_ref[b, turn] - (position - 1) * leaf_dev
        return jnp.minimum(jnp.maximum(number, 0), 3 * leaf_dev - 1)

    def near_weights(b, _):
        @pl.when(ahead + b < leaf_dev)
        def _():
            feed(ahead + b)

        columns = cols[:, pl.ds(pl.multiple_of(b * leaf, leaf), leaf)]
        for turn in range(n_near):
            kept[b, turn * leaf : (turn + 1) * leaf, :] = gaussian(rows[number_of(b, turn)], columns)
        return 0

    send_x(0, partner(1)[1]).wait_recv()
    feed(fed)
    tree_blocks(0, partner(1)[0], partner(2)[1])
    across(0)
    feed(fed + 1)

    @pl.when(has_left)
    def _():
        rightward.wait_recv()

    feed(fed + 2)
    prepare(0)

    @pl.when(has_right)
    def _():
        leftward.wait_recv()

    feed(fed + 3)
    prepare(2 * leaf_dev)
    ahead = fed + 4
    share = max(1, 4 * 4 // (levels - 1))

    def level(k, step):
        _, peer = partner(step)
        bit, peer_above = partner(2 * step)
        def several(i, _):
            for j in range(4):
                near_weights(k * share + 4 * i + j, 0)
            return 0

        lax.fori_loop(0, share // 4, several, 0)
        if share % 4:
            lax.fori_loop(k * share + share // 4 * 4, (k + 1) * share, near_weights, 0)
        send_x(k + 1, peer_above).wait_recv()

        @pl.when(k < levels - 2)
        def _():
            tree_blocks(k + 1, bit, partner(jnp.minimum(4 * step, count // 2))[1])

        across(k + 1)
        part = raised(own_u[k], k, 0, own_blocks[k])
        send_u(k, peer).wait_recv()
        own_u[k + 1] = (part + raised(sib_u[k], k, 1, sib_block[k % 2])).astype(BF16)
        send_u(k + 1, peer_above).start()
        beside[k] = dot(sib_u[k], across_blocks[k % 2])
        return 2 * step

    lax.fori_loop(0, levels - 1, level, jnp.int32(1))
    done = (levels - 1) * share
    if done < leaf_dev:
        lax.fori_loop(done, leaf_dev, near_weights, 0)

    def arrived(j, _):
        @pl.when(has_left)
        def _():
            piece(j, 0).wait_recv()

        @pl.when(has_right)
        def _():
            piece(j, 1).wait_recv()

        return 0

    lax.fori_loop(0, leaf_dev, arrived, 0)

    def near_sum(b, _):
        part = pl.ds(pl.multiple_of(b * leaf, leaf), leaf)
        sides = [leaves_q[number_of(b, turn)] for turn in range(n_near)]
        out_ref[:, part] = dot(jnp.concatenate(sides, 1), kept[b])
        return 0

    lax.fori_loop(0, leaf_dev, near_sum, 0, unroll=8)

    top = levels - 1
    send_u(top, partner(1 << top)[1]).wait_recv()
    down = dot(sib_u[top], across_blocks[top % 2]).astype(BF16)
    for k in range(levels - 2, -1, -1):
        down = (beside[k] + dot(down, own_blocks[k]) * totals[k, 0:1, :]).astype(BF16)

    def store(c):
        return pltpu.make_async_copy(out_ref.at[:, chunk_of(c)], out_hbm.at[:, chunk_of(c)], out_sem.at[c])

    def far(c, _):
        part = chunk_of(c)
        out_ref[:, part] += dot(down, block0[:, part]) * total0[:, part]
        store(c).start()
        return 0

    lax.fori_loop(0, wide, far, 0, unroll=8)

    for k in range(levels):
        peer = partner(1 << k)[1]
        send_x(k, peer).wait_send()
        send_u(k, peer).wait_send()

    for c in range(wide):
        store(c).wait()

    def sent(j, _):
        @pl.when(has_right)
        def _():
            piece(j, 0).wait_send()

        @pl.when(has_left)
        def _():
            piece(j, 1).wait_send()

        return 0

    lax.fori_loop(0, leaf_dev, sent, 0)

    @pl.when(has_right)
    def _():
        rightward.wait_send()

    @pl.when(has_left)
    def _():
        leftward.wait_send()


def body(points, charges, near_leaves, skel_device, skel_tree):
    inner_levels = lax.axis_size("inner").bit_length() - 1
    outer_levels = lax.axis_size("outer").bit_length() - 1
    levels = inner_levels + outer_levels
    n, size = points.shape[1], skel_device.shape[1]
    leaf_dev = near_leaves.shape[0]
    leaf = n // leaf_dev
    coordinates = pltpu.VMEM((levels, DIM, size), BF16)
    loads = pltpu.VMEM((levels, NRHS, size), BF16)
    blocks = pltpu.VMEM((levels, size, size), BF16)
    pair = pltpu.VMEM((2, size, size), BF16)
    each = pltpu.SemaphoreType.DMA((levels,))
    return pl.pallas_call(
        functools.partial(kernel, inner_levels, outer_levels),
        out_shape=jax.ShapeDtypeStruct((NRHS, n), F32),
        in_specs=[pl.BlockSpec(memory_space=pltpu.HBM)] * 5,
        out_specs=pl.BlockSpec(memory_space=pltpu.HBM),
        scratch_shapes=[
            pltpu.SMEM(near_leaves.shape, jnp.int32),
            pltpu.VMEM(skel_device.shape, jnp.int32),
            pltpu.VMEM(skel_tree.shape, jnp.int32),
            pltpu.VMEM((DIM, 3 * n), BF16),
            pltpu.VMEM(charges.shape, BF16),
            pltpu.VMEM((3 * leaf_dev, NRHS, leaf), BF16),
            pltpu.VMEM((3 * leaf_dev, leaf, DEPTH), BF16),
            pltpu.VMEM((DEPTH, n), BF16),
            pltpu.VMEM((size, n), BF16),
            pltpu.VMEM((1, n), F32),
            pltpu.VMEM((NRHS, size), F32),
            coordinates, coordinates, loads, loads, blocks, pair, pair,
            pltpu.VMEM((levels, 2, size), F32),
            pltpu.VMEM((levels, NRHS, size), F32),
            pltpu.VMEM((leaf_dev, near_leaves.shape[1] * leaf, leaf), BF16),
            pltpu.VMEM((NRHS, n), F32),
            pltpu.SemaphoreType.DMA((2,)),
            pltpu.SemaphoreType.DMA((2,)),
            pltpu.SemaphoreType.DMA((2, leaf_dev)),
            pltpu.SemaphoreType.DMA((2, leaf_dev)),
            each, each, each, each,
            pltpu.SemaphoreType.DMA((5,)),
            pltpu.SemaphoreType.DMA((n // 512,)),
        ],
        compiler_params=pltpu.CompilerParams(
            collective_id=0, has_side_effects=True, vmem_limit_bytes=60 << 20
        ),
        name="skeleton_matvec",
    )(near_leaves, points, charges, skel_device, skel_tree)


def solution(mesh):
    return jax.shard_map(
        body,
        mesh=mesh,
        in_specs=(
            P(None, ("outer", "inner")),
            P(None, ("outer", "inner")),
            P(("outer", "inner"), None),
            P(("outer", "inner"), None),
            P(("outer", "inner"), None, None),
        ),
        out_specs=P(None, ("outer", "inner")),
        check_vma=False,
    )
```
